128 devices in a mesh: heads: 4 (over z), ctx: 32 (over y, x, core).
Axes of the slice: x: 4, y: 4, z: 4, core: 2. Of those that a mesh axis runs over, the one named last changes fastest.
Arguments:
- queries: bfloat16 [16384, 2048], P('ctx', 'heads'), may hold values from -6 to 6
- key_heads: bfloat16 [16384, 1024], P('ctx', 'heads'), may hold values from -6 to 6
- value_heads: bfloat16 [16384, 1024], P('ctx', 'heads'), may hold values from -6 to 6
- class_ids: int32 [16384], P('ctx'), may hold values from 0 to 63
- level_table: float32 [64, 16, 9], P(None, 'heads'), may hold values from 0.25 to 2
- out_weight: bfloat16 [2048, 2048], P('ctx', 'heads'), may hold values from -0.125 to 0.125
- out_grad: bfloat16 [16384, 2048], P('ctx', 'heads'), may hold values from -6 to 6
Outputs:
- projected: bfloat16 [16384, 2048], P('ctx', 'heads')
- query_grad: bfloat16 [16384, 2048], P('ctx', 'heads')
- key_grad: bfloat16 [16384, 1024], P('ctx', 'heads')
- value_grad: bfloat16 [16384, 1024], P('ctx', 'heads')
- weight_grad: float32 [2048, 2048], P('ctx', 'heads')
The draws below stay inside these ranges and needn't reach their ends.
All inputs are finite; a program needn't handle non-finite values.
Results may differ from the reference program's by a relative error of at most 0.017.
Values may be sent and summed in bfloat16 or wider, within the bound.
A program may use at most 128 MiB of HBM per device.

```python
import math
import jax
import jax.numpy as jnp
import numpy as np
from jax import lax

D = 2048
H = 16
KV = 8
DH = 128
CH = 64
CLASSES = 64
TOKENS = 16384
LEVELS = 9
N_HEADS = 4


def plant(drawn, key, low, largest):
    place = [jax.random.randint(jax.random.fold_in(key, axis), (), 0, length) for axis, length in enumerate(drawn.shape)]
    longest = drawn.shape.index(max(drawn.shape))
    beside = place[:longest] + [(place[longest] + 1) % drawn.shape[longest]] + place[longest + 1:]
    return drawn.at[tuple(place)].set(low).at[tuple(beside)].set(largest)


def spiked(entries, own_key, source, target, blocks, factor):
    owner, partner = [(jnp.arange(entries.shape[position]) // (entries.shape[position] // blocks)).reshape([-1 if axis == position else 1 for axis in range(entries.ndim)]) for position in (source, target)]
    chosen = jax.random.permutation(own_key, blocks)[partner]
    strong = (owner == chosen) | (owner == (partner + blocks // 2) % blocks)
    return jnp.where(strong, factor * entries, entries)


def level_of(key, extent, shards, least, high):
    factor_of, own = 1.0, jax.random.fold_in(key, 6)
    for axis_at, shards_of in shards:
        draws = jnp.exp(jax.random.uniform(jax.random.fold_in(own, axis_at), (shards_of,), jnp.float32, least / len(shards), high / len(shards)))
        factor_of = factor_of * jnp.repeat(draws, extent[axis_at] // shards_of).reshape([-1 if axis == axis_at else 1 for axis in range(len(extent))])
    return factor_of


def rank_table(count, slope):
    weights = [(1 << 20) // math.isqrt(rank ** slope) + 1 for rank in range(1, count + 1)]
    deviation = 1 + sum(weights) // (1 << 30)
    return np.cumsum(np.array([max(1, weight // deviation) for weight in weights]))


def skewed_ids(stream_key, extent, count, skew):
    grid = rank_table(count, skew)
    lot = jax.random.randint(jax.random.fold_in(stream_key, 1), extent, 0, int(grid[count - 1]))
    rank = jnp.searchsorted(jnp.asarray(grid, jnp.int32), lot, side="right")
    return jax.random.permutation(jax.random.fold_in(stream_key, 2), count)[rank].astype(jnp.int32)


def noise(rng, shape, scale, reach, pieces=(), held_as=jnp.bfloat16):
    loudness = level_of(rng, shape, pieces, -0.22, 0.18) if pieces else 1.0
    result = jax.random.normal(rng, shape, jnp.float32) * scale * loudness
    return jnp.minimum(jnp.maximum(result, -reach), reach).astype(held_as)


def heavy_noise(stream_key, dims, scale, most, pieces, heavy, held_as=jnp.bfloat16):
    values = scale * jax.random.normal(stream_key, dims, jnp.float32)
    if pieces:
        values = values * level_of(stream_key, dims, pieces, -0.22, 0.18)
    return jnp.clip(spiked(values, jax.random.fold_in(stream_key, 3), *heavy), -most, most).astype(held_as)


def setup_inputs(seed: int = 0) -> dict:
    key_list = jax.random.split(jax.random.key(seed), 8)
    return {
        "queries": noise(key_list[0], (TOKENS, H * DH), 1.0, 6.0, ((0, 32), (1, 4))),
        "key_heads": noise(key_list[1], (TOKENS, KV * DH), 1.0, 6.0, ((0, 32), (1, 4))),
        "value_heads": noise(key_list[2], (TOKENS, KV * DH), 1.0, 6.0, ((0, 32), (1, 4))),
        "class_ids": plant(skewed_ids(key_list[3], (TOKENS,), CLASSES, 2), jax.random.fold_in(key_list[3], 3), 0, CLASSES - 1).astype(jnp.int32),
        "level_table": jnp.clip(jnp.exp(math.log(2.0) - 2.0794415 * jax.random.uniform(key_list[4], (CLASSES, H, LEVELS), jnp.float32) ** level_of(key_list[4], (CLASSES, H, LEVELS), ((1, 4),), -0.2, 0.2)), 0.25, 2.0),
        "out_weight": noise(key_list[5], (D, H * DH), (H * DH) ** -0.5, 0.125, ((0, 32), (1, 4))),
        "out_grad": heavy_noise(key_list[6], (TOKENS, D), 1.0, 6.0, ((0, 32), (1, 4)), (0, 1, 32, 2.75)),
    }


def halves(array, pairs, span):
    return array.reshape((pairs, 2, span) + array.shape[1:])


def reference(queries, key_heads, value_heads, class_ids, level_table, out_weight, out_grad):
    total = queries.shape[0]
    stretches = total // CH
    group = H // KV
    shape = (stretches, CH, KV, group, DH)
    query_blocks = queries.reshape(shape).astype(jnp.float32)
    key_blocks = key_heads.reshape(stretches, CH, KV, DH).astype(jnp.float32)
    value_blocks = value_heads.reshape(stretches, CH, KV, DH).astype(jnp.float32)
    lambdas = level_table[class_ids].reshape(stretches, CH, KV, group, LEVELS)

    def coefficient(level):
        return DH ** -0.5 * (CH * 2 ** max(level - 1, 0)) ** -0.5

    def weighted(level):
        return (query_blocks * (coefficient(level) * lambdas[..., level])[..., None]).astype(jnp.bfloat16)

    grad_attn = jnp.dot(out_grad, out_weight, preferred_element_type=jnp.float32).astype(jnp.bfloat16)
    grad_blocks = grad_attn.reshape(shape).astype(jnp.float32)

    mask = jnp.tril(jnp.ones((CH, CH), dtype=bool))
    first = weighted(0).astype(jnp.float32)
    raw = jnp.einsum('cigrd,cjgd->cgrij', first, key_blocks)
    scores = jnp.where(mask, raw, 0.0).astype(jnp.bfloat16).astype(jnp.float32)
    output = jnp.einsum('cgrij,cjge->cigre', scores, value_blocks)
    grad_raw = jnp.einsum('cigre,cjge->cgrij', grad_blocks, value_blocks)
    grad_scores = jnp.where(mask, grad_raw, 0.0).astype(jnp.bfloat16).astype(jnp.float32)
    grad_query = (coefficient(0) * lambdas[..., 0])[..., None] * jnp.einsum('cgrij,cjgd->cigrd', grad_scores, key_blocks)
    grad_key = jnp.einsum('cgrij,cigrd->cjgd', grad_scores, first)
    grad_value = jnp.einsum('cgrij,cigre->cjge', scores, grad_blocks)

    stretch_states = jnp.einsum('cjgd,cjge->cgde', key_blocks, value_blocks)
    key_side = jnp.zeros((stretches, KV, DH, DH), jnp.float32)
    for height in range(LEVELS - 1):
        level = height + 1
        span = 1 << height
        pairs = stretches >> (height + 1)
        upper_q = halves(weighted(level).astype(jnp.float32), pairs, span)[:, 1]
        upper_grad = halves(grad_blocks, pairs, span)[:, 1]
        upper_scale = halves(coefficient(level) * lambdas[..., level], pairs, span)[:, 1]
        lower = halves(stretch_states, pairs, span)[:, 0].sum(axis=1)
        lower = lower.astype(jnp.bfloat16).astype(jnp.float32)
        read = jnp.einsum('nsigrd,ngde->nsigre', upper_q, lower)
        back = upper_scale[..., None] * jnp.einsum('nsigre,ngde->nsigrd', upper_grad, lower)
        output = output + jnp.stack([jnp.zeros_like(read), read], axis=1).reshape(shape)
        grad_query = grad_query + jnp.stack([jnp.zeros_like(back), back], axis=1).reshape(shape)
        state_grad = jnp.einsum('nsigrd,nsigre->ngde', upper_q, upper_grad)
        spread = jnp.broadcast_to(state_grad[:, None], (pairs, span, KV, DH, DH))
        key_side = key_side + jnp.stack([spread, jnp.zeros_like(spread)], axis=1).reshape(stretches, KV, DH, DH)
    key_side = key_side.astype(jnp.bfloat16).astype(jnp.float32)
    grad_key = grad_key + jnp.einsum('cjge,cgde->cjgd', value_blocks, key_side)
    grad_value = grad_value + jnp.einsum('cjgd,cgde->cjge', key_blocks, key_side)

    attn = output.astype(jnp.bfloat16).reshape(total, H * DH)
    width = H * DH // N_HEADS
    projected = jnp.zeros((total, D), jnp.float32)
    for block in range(N_HEADS):
        part = lax.dot_general(attn[:, block * width:(block + 1) * width], out_weight[:, block * width:(block + 1) * width], (((1,), (1,)), ((), ())), preferred_element_type=jnp.float32)
        projected = projected + lax.optimization_barrier(part.astype(jnp.bfloat16)).astype(jnp.float32)
    weight_grad = lax.dot_general(out_grad, attn, (((0,), (0,)), ((), ())), preferred_element_type=jnp.float32) * (TOKENS ** -0.5)
    return (projected.astype(jnp.bfloat16),
            grad_query.astype(jnp.bfloat16).reshape(total, H * DH),
            grad_key.astype(jnp.bfloat16).reshape(total, KV * DH),
            grad_value.astype(jnp.bfloat16).reshape(total, KV * DH),
            weight_grad)
```

```python
import jax
import jax.numpy as jnp
from jax import lax
from jax.experimental import pallas as pl
from jax.experimental.pallas import tpu as pltpu
from jax.sharding import PartitionSpec as P

DH = 128
CH = 64
RING = 4
LOCAL = 4
CROSS = 5
TILE = 256
TOKENS = 512
WIDTH = 512
HEADS = 4
GROUPS = 2
BF16 = jnp.bfloat16
F32 = jnp.float32


def coefficient(level):
    return DH ** (-0.5) * (CH * 2 ** max(level - 1, 0)) ** (-0.5)


def contract(a, b, da, db, precision=None):
    return lax.dot_general(
        a, b, (((da,), (db,)), ((), ())), preferred_element_type=F32, precision=precision
    )


def dot(a, b):
    return contract(a, b, 1, 0)


def dot_nt(a, b):
    return contract(a, b, 1, 1)


def dot_tn(a, b):
    return contract(a, b, 0, 0)


def ring(index, offset):
    return lax.rem(index + offset + RING, RING)


def flag(condition):
    return condition.astype(jnp.int32).astype(F32)


def make_kernel(norm):
    def kernel(
        q_ref, k_ref, v_ref, ids_ref, tab_ref, w_ref, og_ref,
        proj_ref, dq_ref, dk_ref, dv_ref, wg_ref,
        ogf, wf, acc, attn, ga, piece, zbuf, wg, wgc, ybuf, xpiece, xbuf,
        scale, wqc, prob, total, ssend, srecv, read, gmat, gacc, gsend, grecv, dka, dva,
        ssem, rsem,
    ):
        z = lax.axis_index("heads")
        c = lax.axis_index("ctx")
        core = lax.rem(c, 2)
        x = lax.rem(c // 2, RING)
        y = c // 8
        used = [0]
        sent = []

        def z_dev(offset):
            return {"heads": ring(z, offset)}

        def x_dev(offset):
            return {"ctx": (y * RING + ring(x, offset)) * 2 + core}

        def y_dev(offset):
            return {"ctx": (ring(y, offset) * RING + x) * 2 + core}

        sibling = {"ctx": (y * RING + x) * 2 + 1 - core}

        def send(src, dst, device):
            number = used[0]
            used[0] = number + 1
            copy = pltpu.make_async_remote_copy(
                src_ref=src,
                dst_ref=dst,
                send_sem=ssem.at[number],
                recv_sem=rsem.at[number],
                device_id=device,
                device_id_type=pl.DeviceIdType.MESH,
            )
            copy.start()
            sent.append(copy)
            return copy

        def gather_start(dev, index, half):
            right, left = dev(1), dev(-1)
            a = send(half(index, 0), half(index, 0), right)
            b = send(half(index, 1), half(index, 1), left)
            d = send(half(index, 1), half(index, 1), right)
            e = send(half(index, 0), half(index, 0), left)
            return a, b, d, e

        def gather_forward(dev, index, half, copies):
            before, after = ring(index, -1), ring(index, 1)
            copies[0].wait_recv()
            a = send(half(before, 0), half(before, 0), dev(1))
            copies[1].wait_recv()
            b = send(half(after, 1), half(after, 1), dev(-1))
            return a, b

        def scatter_far(dev, index, half, buf):
            far = ring(index, 2)
            return (
                send(half(far, 0), buf.at[0], dev(1)),
                send(half(far, 1), buf.at[3], dev(-1)),
            )

        def scatter_near(dev, index, half, buf):
            return (
                send(half(ring(index, 1), 1), buf.at[1], dev(1)),
                send(half(ring(index, -1), 0), buf.at[4], dev(-1)),
            )

        def scatter_middle(dev, index, half, buf, far):
            after, before = half(ring(index, 1), 0), half(ring(index, -1), 1)
            far[0].wait_recv()
            after[...] = (after[...].astype(F32) + buf[0].astype(F32)).astype(BF16)
            a = send(after, buf.at[2], dev(1))
            far[1].wait_recv()
            before[...] = (before[...].astype(F32) + buf[3].astype(F32)).astype(BF16)
            b = send(before, buf.at[5], dev(-1))
            return a, b

        def scatter_wait(near, middle):
            for copy in near + middle:
                copy.wait_recv()

        def scatter_sum(index, half, buf, part):
            own = half(index, part)[...].astype(F32)
            if part == 0:
                return own + buf[2].astype(F32) + buf[4].astype(F32)
            return own + buf[1].astype(F32) + buf[5].astype(F32)

        barrier = pltpu.get_barrier_semaphore()
        peers = [z_dev(1), z_dev(-1), sibling]
        for offset in (1, 2, 3):
            peers += [x_dev(offset), y_dev(offset)]
        for device in peers:
            pl.semaphore_signal(
                barrier, inc=1, device_id=device, device_id_type=pl.DeviceIdType.MESH
            )
        pl.semaphore_wait(barrier, len(peers))

        def og_half(block, part):
            return ogf.at[block, pl.ds(part * TILE, TILE)]

        ogf[z] = og_ref[...]
        og_copies = gather_start(z_dev, z, og_half)

        own = y * RING + x
        wf[own, core] = w_ref[...]
        w_x = [send(wf.at[own, core], wf.at[own, core], x_dev(o)) for o in (1, 3, 2)]

        for g in range(GROUPS):
            cols = slice(g * DH, (g + 1) * DH)
            total[g] = dot_tn(k_ref[:, cols], v_ref[:, cols])
        ssend[0] = total[...].astype(BF16)
        s_core = send(ssend.at[0], srecv.at[0], sibling)

        classes = tab_ref.shape[0]
        onehot = (
            lax.broadcasted_iota(jnp.int32, (classes, TOKENS), 0) == ids_ref[...]
        ).astype(F32)
        levels = LOCAL + CROSS
        level = lax.broadcasted_iota(jnp.int32, (1, levels), 1)
        coef = jnp.full((1, levels), coefficient(0), F32)
        for number in range(1, levels):
            coef = jnp.where(level == number, coefficient(number), coef)
        for h in range(HEADS):
            lam = contract(onehot, tab_ref[:, h, :], 0, 0, lax.Precision.HIGHEST)
            scale[h] = lam * coef

        def w_half(block, part):
            return wf.at[pl.ds(block * RING + part * 2, 2), core]

        def w_row(block):
            return wf.at[pl.ds(block * RING, RING), core]

        for copy in w_x:
            copy.wait_recv()
        w_y = gather_start(y_dev, y, w_half)
        w_rows = [send(w_row(y), w_row(y), sibling)]

        s_core.wait_recv()
        got = srecv[0].astype(F32)
        for g in range(GROUPS):
            read[g, 0:DH] = (got[g] * flag(core == 1)).astype(BF16)
        total[...] += got
        ssend[1] = total[...].astype(BF16)
        s_x = [send(ssend.at[1], srecv.at[o], x_dev(o)) for o in (1, 2, 3)]

        def weigh(h):
            cols = pl.ds(pl.multiple_of(h * DH, DH), DH)
            q = q_ref[:, cols].astype(F32)
            for l in range(CROSS):
                wqc[h, :, l * DH : (l + 1) * DH] = (
                    q * scale[h, :, LOCAL + l : LOCAL + l + 1]
                ).astype(BF16)

        lax.fori_loop(0, HEADS, lambda h, _: (weigh(h), 0)[1], 0)

        og_far = gather_forward(z_dev, z, og_half, og_copies)

        def exchange(copies, position, slot, low):
            near = jnp.zeros((GROUPS, DH, DH), F32)
            far = jnp.zeros((GROUPS, DH, DH), F32)
            everything = total[...]
            for o, copy in zip((1, 2, 3), copies):
                copy.wait_recv()
                source = ring(position, -o)
                value = srecv[slot + o].astype(F32)
                upper = source < position
                same = source // 2 == position // 2
                near += value * flag(jnp.logical_and(upper, same))
                far += value * flag(jnp.logical_and(upper, jnp.logical_not(same)))
                everything += value
            for g in range(GROUPS):
                read[g, low * DH : (low + 1) * DH] = near[g].astype(BF16)
                read[g, (low + 1) * DH : (low + 2) * DH] = far[g].astype(BF16)
            total[...] = everything

        exchange(s_x, x, 0, 1)
        ssend[2] = total[...].astype(BF16)
        s_y = [send(ssend.at[2], srecv.at[3 + o], y_dev(o)) for o in (1, 2, 3)]

        rows = lax.broadcasted_iota(jnp.int32, (TILE, TILE), 0)
        cols_ = lax.broadcasted_iota(jnp.int32, (TILE, TILE), 1)

        def tile_weight(h, i):
            span = pl.ds(i * TILE, TILE)
            weight = jnp.where(
                rows // (2 * CH) > cols_ // (2 * CH), scale[h, span, 2:3], 0.0
            )
            weight = jnp.where(
                jnp.logical_and(
                    rows // (2 * CH) == cols_ // (2 * CH), rows // CH > cols_ // CH
                ),
                scale[h, span, 1:2],
                weight,
            )
            return jnp.where(
                jnp.logical_and(rows // CH == cols_ // CH, rows >= cols_),
                scale[h, span, 0:1],
                weight,
            )

        first, second = pl.ds(0, TILE), pl.ds(TILE, TILE)

        def forward(h):
            cols = pl.ds(pl.multiple_of(h * DH, DH), DH)
            group = pl.ds(pl.multiple_of(h // 2 * DH, DH), DH)
            q0, q1 = q_ref[first, cols], q_ref[second, cols]
            k0, k1 = k_ref[first, group], k_ref[second, group]
            v0, v1 = v_ref[first, group], v_ref[second, group]
            p0 = (dot_nt(q0, k0) * tile_weight(h, 0)).astype(BF16)
            p1 = (dot_nt(q1, k1) * tile_weight(h, 1)).astype(BF16)
            p2 = (dot_nt(q1, k0) * scale[h, second, 3:4]).astype(BF16)
            prob[h, 0] = p0
            prob[h, 1] = p1
            prob[h, 2] = p2
            acc[first, cols] = dot(p0, v0)
            acc[second, cols] = dot(p1, v1) + dot(p2, v0)

        lax.fori_loop(0, 2, lambda h, _: (forward(h), 0)[1], 0)
        w_far = gather_forward(y_dev, y, w_half, w_y)
        lax.fori_loop(2, HEADS, lambda h, _: (forward(h), 0)[1], 0)
        w_y[2].wait_recv()
        w_rows.append(send(w_row(ring(y, -1)), w_row(ring(y, -1)), sibling))
        w_y[3].wait_recv()
        w_rows.append(send(w_row(ring(y, 1)), w_row(ring(y, 1)), sibling))
        exchange(s_y, y, 3, 3)

        def across(h):
            cols = pl.ds(pl.multiple_of(h * DH, DH), DH)
            attn[:, cols] = (acc[:, cols] + dot(wqc[h], read[h // 2])).astype(BF16)

        lax.fori_loop(0, HEADS, lambda h, _: (across(h), 0)[1], 0)
        w_far[0].wait_recv()
        w_far[1].wait_recv()
        w_rows.append(send(w_row(ring(y, 2)), w_row(ring(y, 2)), sibling))
        for copy in w_rows:
            copy.wait_recv()

        def weights(block):
            return wf[pl.ds(block * RING, RING)].reshape(WIDTH, WIDTH)

        def project(block):
            def step(t, _):
                span = pl.ds(pl.multiple_of(t * TILE, TILE), TILE)
                piece[block, span] = dot_nt(attn[span], weights(block)).astype(BF16)
                return 0

            lax.fori_loop(0, 2, step, 0)

        def z_half(block, part):
            return piece.at[block, pl.ds(part * TILE, TILE)]

        project(ring(z, 2))
        z_far = scatter_far(z_dev, z, z_half, zbuf)
        project(ring(z, 1))
        project(ring(z, -1))
        z_near = scatter_near(z_dev, z, z_half, zbuf)

        def back(block, start):
            def step(t, _):
                span = pl.ds(pl.multiple_of(t * TILE, TILE), TILE)
                term = dot(ogf[block, span], weights(block))
                acc[span] = term if start else acc[span] + term
                return 0

            lax.fori_loop(0, 2, step, 0)

        wg_core = []

        def weight_grad(block):
            def step(t, _):
                span = pl.ds(pl.multiple_of(t * TILE, TILE), TILE)
                term = dot_tn(ogf[block, :, span], attn[...]).astype(BF16)
                wg[pl.ds(block * RING + t * 2, 2)] = term.reshape(2, 2, CH, WIDTH)
                return 0

            lax.fori_loop(0, 2, step, 0)
            span = pl.ds(block * RING, RING)
            wg_core.append(send(wg.at[span, 1 - core], wgc.at[span], sibling))

        back(z, True)
        weight_grad(z)
        project(z)
        og_copies[2].wait_recv()
        back(ring(z, -1), False)
        og_copies[3].wait_recv()
        back(ring(z, 1), False)
        weight_grad(ring(z, -1))
        weight_grad(ring(z, 1))
        og_far[0].wait_recv()
        og_far[1].wait_recv()
        back(ring(z, 2), False)
        ga[...] = acc[...].astype(BF16)
        z_middle = scatter_middle(z_dev, z, z_half, zbuf, z_far)
        weight_grad(ring(z, 2))

        def state_grad(g):
            value = jnp.zeros((DH, CROSS * DH), F32)
            for r in range(2):
                h = g * 2 + r
                cols = pl.ds(pl.multiple_of(h * DH, DH), DH)
                value += dot_tn(ga[:, cols], wqc[h])
            gmat[g] = value

        lax.fori_loop(0, GROUPS, lambda g, _: (state_grad(g), 0)[1], 0)

        def level_grad(number):
            return gmat[:, :, number * DH : (number + 1) * DH]

        g_y = []
        for o in (1, 2, 3):
            same = flag(y // 2 == ring(y, o) // 2)
            gsend[o] = (level_grad(3) * same + level_grad(4) * (1.0 - same)).astype(BF16)
            g_y.append(send(gsend.at[o], grecv.at[o], y_dev(o)))

        for copy in wg_core:
            copy.wait_recv()

        def merge(t, _):
            wgc[t] = (wg[t, core].astype(F32) + wgc[t].astype(F32)).astype(BF16)
            return 0

        lax.fori_loop(0, RING * RING, merge, 0)

        def y_half(block, part):
            return wgc.at[pl.ds(block * RING + part * 2, 2)]

        y_far = scatter_far(y_dev, y, y_half, ybuf)
        y_near = scatter_near(y_dev, y, y_half, ybuf)

        def backward(g):
            group = pl.ds(pl.multiple_of(g * DH, DH), DH)
            k0, k1 = k_ref[first, group], k_ref[second, group]
            v0, v1 = v_ref[first, group], v_ref[second, group]
            for r in range(2):
                h = g * 2 + r
                cols = pl.ds(pl.multiple_of(h * DH, DH), DH)
                q0, q1 = q_ref[first, cols], q_ref[second, cols]
                g0, g1 = ga[first, cols], ga[second, cols]
                d0 = (dot_nt(g0, v0) * tile_weight(h, 0)).astype(BF16)
                d1 = (dot_nt(g1, v1) * tile_weight(h, 1)).astype(BF16)
                d2 = (dot_nt(g1, v0) * scale[h, second, 3:4]).astype(BF16)
                dq0 = dot(d0, k0)
                dq1 = dot(d1, k1) + dot(d2, k0)
                y0, y1 = dot_nt(g0, read[g]), dot_nt(g1, read[g])
                for l in range(CROSS):
                    part = slice(l * DH, (l + 1) * DH)
                    number = slice(LOCAL + l, LOCAL + l + 1)
                    dq0 += y0[:, part] * scale[h, first, number]
                    dq1 += y1[:, part] * scale[h, second, number]
                dq_ref[first, cols] = dq0.astype(BF16)
                dq_ref[second, cols] = dq1.astype(BF16)
                p0, p1, p2 = prob[h, 0], prob[h, 1], prob[h, 2]
                dk0 = dot_tn(d0, q0) + dot_tn(d2, q1)
                dk1 = dot_tn(d1, q1)
                dv0 = dot_tn(p0, g0) + dot_tn(p2, g1)
                dv1 = dot_tn(p1, g1)
                if r == 0:
                    dka[first, group] = dk0
                    dka[second, group] = dk1
                    dva[first, group] = dv0
                    dva[second, group] = dv1
                else:
                    dka[first, group] += dk0
                    dka[second, group] += dk1
                    dva[first, group] += dv0
                    dva[second, group] += dv1

        backward_loop = lambda a, b: lax.fori_loop(a, b, lambda g, _: (backward(g), 0)[1], 0)
        backward_loop(0, 1)

        y_middle = scatter_middle(y_dev, y, y_half, ybuf, y_far)
        gacc[...] = jnp.zeros_like(gacc)
        for o, copy in zip((1, 2, 3), g_y):
            copy.wait_recv()
            gacc[...] += grecv[o].astype(F32) * flag(ring(y, -o) > y)
        g_x = []
        for o in (1, 2, 3):
            same = flag(x // 2 == ring(x, o) // 2)
            lower = flag(x > ring(x, o))
            gsend[3 + o] = (
                gacc[...]
                + level_grad(1) * (lower * same)
                + level_grad(2) * (lower * (1.0 - same))
            ).astype(BF16)
            g_x.append(send(gsend.at[3 + o], grecv.at[3 + o], x_dev(o)))
        backward_loop(1, 2)
        for o, copy in zip((1, 2, 3), g_x):
            copy.wait_recv()
            gacc[...] += grecv[3 + o].astype(F32)
        gsend[0] = (gacc[...] + level_grad(0) * flag(core == 1)).astype(BF16)
        g_core = send(gsend.at[0], grecv.at[0], sibling)

        scatter_wait(y_near, y_middle)
        xpiece[0:2] = scatter_sum(y, y_half, ybuf, 0).astype(BF16)
        xpiece[2:4] = scatter_sum(y, y_half, ybuf, 1).astype(BF16)

        def x_half(block, part):
            return xpiece.at[block, pl.ds(part * 32, 32)]

        x_far = scatter_far(x_dev, x, x_half, xbuf)
        x_near = scatter_near(x_dev, x, x_half, xbuf)

        g_core.wait_recv()
        gacc[...] += grecv[0].astype(F32)
        for g in range(GROUPS):
            cols = slice(g * DH, (g + 1) * DH)
            key_side = gacc[g].astype(BF16)
            dk_ref[:, cols] = (dka[:, cols] + dot(v_ref[:, cols], key_side)).astype(BF16)
            dv_ref[:, cols] = (dva[:, cols] + dot_nt(k_ref[:, cols], key_side)).astype(BF16)

        x_middle = scatter_middle(x_dev, x, x_half, xbuf, x_far)
        scatter_wait(x_near, x_middle)
        wg_ref[0:32] = scatter_sum(x, x_half, xbuf, 0) * norm
        wg_ref[32:64] = scatter_sum(x, x_half, xbuf, 1) * norm

        scatter_wait(z_near, z_middle)
        proj_ref[0:TILE] = scatter_sum(z, z_half, zbuf, 0).astype(BF16)
        proj_ref[TILE:] = scatter_sum(z, z_half, zbuf, 1).astype(BF16)
        for copy in sent:
            copy.wait_send()

    return kernel


COPIES = 60


def local(queries, key_heads, value_heads, class_ids, level_table, out_weight, out_grad):
    tokens = queries.shape[0]
    norm = (tokens * lax.axis_size("ctx")) ** (-0.5)
    levels = LOCAL + CROSS
    vmem = pl.BlockSpec(memory_space=pltpu.VMEM)
    scratch = [
        pltpu.VMEM((RING, TOKENS, WIDTH), BF16),
        pltpu.VMEM((RING * RING, 2, CH, WIDTH), BF16),
        pltpu.VMEM((TOKENS, WIDTH), F32),
        pltpu.VMEM((TOKENS, WIDTH), BF16),
        pltpu.VMEM((TOKENS, WIDTH), BF16),
        pltpu.VMEM((RING, TOKENS, WIDTH), BF16),
        pltpu.VMEM((6, TILE, WIDTH), BF16),
        pltpu.VMEM((RING * RING, 2, CH, WIDTH), BF16),
        pltpu.VMEM((RING * RING, CH, WIDTH), BF16),
        pltpu.VMEM((6, 2, CH, WIDTH), BF16),
        pltpu.VMEM((RING, CH, WIDTH), BF16),
        pltpu.VMEM((6, 32, WIDTH), BF16),
        pltpu.VMEM((HEADS, TOKENS, levels), F32),
        pltpu.VMEM((HEADS, TOKENS, CROSS * DH), BF16),
        pltpu.VMEM((HEADS, 3, TILE, TILE), BF16),
        pltpu.VMEM((GROUPS, DH, DH), F32),
        pltpu.VMEM((3, GROUPS, DH, DH), BF16),
        pltpu.VMEM((7, GROUPS, DH, DH), BF16),
        pltpu.VMEM((GROUPS, CROSS * DH, DH), BF16),
        pltpu.VMEM((GROUPS, DH, CROSS * DH), F32),
        pltpu.VMEM((GROUPS, DH, DH), F32),
        pltpu.VMEM((7, GROUPS, DH, DH), BF16),
        pltpu.VMEM((7, GROUPS, DH, DH), BF16),
        pltpu.VMEM((TOKENS, GROUPS * DH), F32),
        pltpu.VMEM((TOKENS, GROUPS * DH), F32),
        pltpu.SemaphoreType.DMA((COPIES,)),
        pltpu.SemaphoreType.DMA((COPIES,)),
    ]
    return pl.pallas_call(
        make_kernel(norm),
        out_shape=(
            jax.ShapeDtypeStruct((TOKENS, WIDTH), BF16),
            jax.ShapeDtypeStruct((TOKENS, WIDTH), BF16),
            jax.ShapeDtypeStruct((TOKENS, GROUPS * DH), BF16),
            jax.ShapeDtypeStruct((TOKENS, GROUPS * DH), BF16),
            jax.ShapeDtypeStruct((CH, WIDTH), F32),
        ),
        in_specs=[vmem] * 7,
        out_specs=(vmem,) * 5,
        scratch_shapes=scratch,
        compiler_params=pltpu.CompilerParams(
            collective_id=0, has_side_effects=True, vmem_limit_bytes=56 << 20
        ),
        name="layer",
    )(
        queries,
        key_heads,
        value_heads,
        class_ids.reshape(1, tokens),
        level_table,
        out_weight,
        out_grad,
    )


def solution(mesh):
    placed = (
        P("ctx", "heads"),
        P("ctx", "heads"),
        P("ctx", "heads"),
        P("ctx"),
        P(None, "heads", None),
        P("ctx", "heads"),
        P("ctx", "heads"),
    )
    return jax.shard_map(
        local,
        mesh=mesh,
        in_specs=placed,
        out_specs=(P("ctx", "heads"),) * 5,
        check_vma=False,
    )
```

```python
import jax
import jax.numpy as jnp
from jax import lax
from jax.experimental import pallas as pl
from jax.experimental.pallas import tpu as pltpu
from jax.sharding import PartitionSpec as P

DH = 128
CH = 64
RING = 4
LOCAL = 4
CROSS = 5
TILE = 256
TOKENS = 512
WIDTH = 512
HEADS = 4
GROUPS = 2
BF16 = jnp.bfloat16
F32 = jnp.float32


def coefficient(level):
    return DH ** (-0.5) * (CH * 2 ** max(level - 1, 0)) ** (-0.5)


def contract(a, b, da, db, precision=None):
    return lax.dot_general(
        a, b, (((da,), (db,)), ((), ())), preferred_element_type=F32, precision=precision
    )


def dot(a, b):
    return contract(a, b, 1, 0)


def dot_nt(a, b):
    return contract(a, b, 1, 1)


def dot_tn(a, b):
    return contract(a, b, 0, 0)


def ring(index, offset):
    return lax.rem(index + offset + RING, RING)


def flag(condition):
    return condition.astype(jnp.int32).astype(F32)


def make_kernel(norm):
    def kernel(
        q_hbm, k_hbm, v_hbm, ids_ref, tab_ref, w_hbm, og_hbm,
        proj_ref, dq_ref, dk_ref, dv_ref, wg_ref,
        q_ref, k_ref, v_ref, ogf, wf, acc, attn, ga, piece, zbuf, wg, wgc, buf1, half2, buf2,
        scale, wqc, prob, total, ssend, srecv, read, gmat, gacc, gsend, grecv, dka, dva,
        lsem, ssem, rsem,
    ):
        z = lax.axis_index("heads")
        c = lax.axis_index("ctx")
        core = lax.rem(c, 2)
        x = lax.rem(c // 2, RING)
        y = c // 8
        used = [0]
        sent = []

        def z_dev(offset):
            return {"heads": ring(z, offset)}

        def x_dev(offset):
            return {"ctx": (y * RING + ring(x, offset)) * 2 + core}

        def y_dev(offset):
            return {"ctx": (ring(y, offset) * RING + x) * 2 + core}

        sibling = {"ctx": (y * RING + x) * 2 + 1 - core}

        def send(src, dst, device):
            number = used[0]
            used[0] = number + 1
            copy = pltpu.make_async_remote_copy(
                src_ref=src,
                dst_ref=dst,
                send_sem=ssem.at[number],
                recv_sem=rsem.at[number],
                device_id=device,
                device_id_type=pl.DeviceIdType.MESH,
            )
            copy.start()
            sent.append(copy)
            return copy

        def gather_start(dev, index, half):
            right, left = dev(1), dev(-1)
            a = send(half(index, 0), half(index, 0), right)
            b = send(half(index, 1), half(index, 1), left)
            d = send(half(index, 1), half(index, 1), right)
            e = send(half(index, 0), half(index, 0), left)
            return a, b, d, e

        def gather_forward(dev, index, half, copies):
            before, after = ring(index, -1), ring(index, 1)
            copies[0].wait_recv()
            a = send(half(before, 0), half(before, 0), dev(1))
            copies[1].wait_recv()
            b = send(half(after, 1), half(after, 1), dev(-1))
            return a, b

        def scatter_far(dev, index, half, buf):
            far = ring(index, 2)
            return (
                send(half(far, 0), buf.at[0], dev(1)),
                send(half(far, 1), buf.at[3], dev(-1)),
            )

        def scatter_near(dev, index, half, buf):
            return (
                send(half(ring(index, 1), 1), buf.at[1], dev(1)),
                send(half(ring(index, -1), 0), buf.at[4], dev(-1)),
            )

        def scatter_middle(dev, index, half, buf, far):
            after, before = half(ring(index, 1), 0), half(ring(index, -1), 1)
            far[0].wait_recv()
            after[...] = (after[...].astype(F32) + buf[0].astype(F32)).astype(BF16)
            a = send(after, buf.at[2], dev(1))
            far[1].wait_recv()
            before[...] = (before[...].astype(F32) + buf[3].astype(F32)).astype(BF16)
            b = send(before, buf.at[5], dev(-1))
            return a, b

        def scatter_wait(near, middle):
            for copy in near + middle:
                copy.wait_recv()

        def scatter_sum(index, half, buf, part):
            own = half(index, part)[...].astype(F32)
            if part == 0:
                return own + buf[2].astype(F32) + buf[4].astype(F32)
            return own + buf[1].astype(F32) + buf[5].astype(F32)

        barrier = pltpu.get_barrier_semaphore()
        peers = [z_dev(1), z_dev(-1), sibling]
        for offset in (1, 2, 3):
            peers += [x_dev(offset), y_dev(offset)]
        for device in peers:
            pl.semaphore_signal(
                barrier, inc=1, device_id=device, device_id_type=pl.DeviceIdType.MESH
            )

        fetched = [
            pltpu.make_async_copy(source, target, lsem.at[i])
            for i, (source, target) in enumerate(
                (
                    (og_hbm, ogf.at[z]),
                    (w_hbm, wf.at[y, x, core]),
                    (k_hbm, k_ref),
                    (v_hbm, v_ref),
                    (q_hbm, q_ref),
                )
            )
        ]
        for copy in fetched:
            copy.start()
        for copy in fetched:
            copy.wait()
        pl.semaphore_wait(barrier, len(peers))

        def og_half(block, part):
            return ogf.at[block, pl.ds(part * TILE, TILE)]

        og_copies = gather_start(z_dev, z, og_half)

        left, right = pl.ds(0, TILE), pl.ds(TILE, TILE)
        mine_l = wf.at[y, x, core, :, left]
        mine_r = wf.at[y, x, core, :, right]
        w_one = [send(mine_l, mine_l, x_dev(o)) for o in (1, 3, 2)]
        w_one += [send(mine_r, mine_r, y_dev(o)) for o in (1, 3, 2)]

        for g in range(GROUPS):
            cols = slice(g * DH, (g + 1) * DH)
            total[g] = dot_tn(k_ref[:, cols], v_ref[:, cols])
        ssend[0] = total[...].astype(BF16)
        s_core = send(ssend.at[0], srecv.at[0], sibling)

        classes = tab_ref.shape[2]
        onehot = (
            lax.broadcasted_iota(jnp.int32, (classes, TOKENS), 0) == ids_ref[...]
        ).astype(F32)
        levels = LOCAL + CROSS
        level = lax.broadcasted_iota(jnp.int32, (1, levels), 1)
        coef = jnp.full((1, levels), coefficient(0), F32)
        for number in range(1, levels):
            coef = jnp.where(level == number, coefficient(number), coef)
        for h in range(HEADS):
            lam = contract(onehot, tab_ref[:, h, :], 0, 1, lax.Precision.HIGHEST)
            scale[h] = lam * coef

        for copy in w_one:
            copy.wait_recv()
        row_l = wf.at[y, :, core, :, left]
        row_r = wf.at[:, x, core, :, right]
        w_two_l = [send(row_l, row_l, y_dev(o)) for o in (1, 3, 2)]
        w_two_r = [send(row_r, row_r, x_dev(o)) for o in (1, 3, 2)]

        s_core.wait_recv()
        got = srecv[0].astype(F32)
        for g in range(GROUPS):
            read[g, 0:DH] = (got[g] * flag(core == 1)).astype(BF16)
        total[...] += got
        ssend[1] = total[...].astype(BF16)
        s_x = [send(ssend.at[1], srecv.at[o], x_dev(o)) for o in (1, 2, 3)]

        def weigh(h):
            cols = pl.ds(pl.multiple_of(h * DH, DH), DH)
            q = q_ref[:, cols].astype(F32)
            for l in range(CROSS):
                wqc[h, :, l * DH : (l + 1) * DH] = (
                    q * scale[h, :, LOCAL + l : LOCAL + l + 1]
                ).astype(BF16)

        lax.fori_loop(0, HEADS, lambda h, _: (weigh(h), 0)[1], 0)

        og_far = gather_forward(z_dev, z, og_half, og_copies)

        def exchange(copies, position, slot, low):
            near = jnp.zeros((GROUPS, DH, DH), F32)
            far = jnp.zeros((GROUPS, DH, DH), F32)
            everything = total[...]
            for o, copy in zip((1, 2, 3), copies):
                copy.wait_recv()
                source = ring(position, -o)
                value = srecv[slot + o].astype(F32)
                upper = source < position
                same = source // 2 == position // 2
                near += value * flag(jnp.logical_and(upper, same))
                far += value * flag(jnp.logical_and(upper, jnp.logical_not(same)))
                everything += value
            for g in range(GROUPS):
                read[g, low * DH : (low + 1) * DH] = near[g].astype(BF16)
                read[g, (low + 1) * DH : (low + 2) * DH] = far[g].astype(BF16)
            total[...] = everything

        exchange(s_x, x, 0, 1)
        ssend[2] = total[...].astype(BF16)
        s_y = [send(ssend.at[2], srecv.at[3 + o], y_dev(o)) for o in (1, 2, 3)]

        rows = lax.broadcasted_iota(jnp.int32, (TILE, TILE), 0)
        cols_ = lax.broadcasted_iota(jnp.int32, (TILE, TILE), 1)

        def tile_weight(h, i):
            span = pl.ds(i * TILE, TILE)
            weight = jnp.where(
                rows // (2 * CH) > cols_ // (2 * CH), scale[h, span, 2:3], 0.0
            )
            weight = jnp.where(
                jnp.logical_and(
                    rows // (2 * CH) == cols_ // (2 * CH), rows // CH > cols_ // CH
                ),
                scale[h, span, 1:2],
                weight,
            )
            return jnp.where(
                jnp.logical_and(rows // CH == cols_ // CH, rows >= cols_),
                scale[h, span, 0:1],
                weight,
            )

        first, second = pl.ds(0, TILE), pl.ds(TILE, TILE)

        def forward(h):
            cols = pl.ds(pl.multiple_of(h * DH, DH), DH)
            group = pl.ds(pl.multiple_of(h // 2 * DH, DH), DH)
            q0, q1 = q_ref[first, cols], q_ref[second, cols]
            k0, k1 = k_ref[first, group], k_ref[second, group]
            v0, v1 = v_ref[first, group], v_ref[second, group]
            p0 = (dot_nt(q0, k0) * tile_weight(h, 0)).astype(BF16)
            p1 = (dot_nt(q1, k1) * tile_weight(h, 1)).astype(BF16)
            p2 = (dot_nt(q1, k0) * scale[h, second, 3:4]).astype(BF16)
            prob[h, 0] = p0
            prob[h, 1] = p1
            prob[h, 2] = p2
            acc[first, cols] = dot(p0, v0)
            acc[second, cols] = dot(p1, v1) + dot(p2, v0)

        lax.fori_loop(0, HEADS, lambda h, _: (forward(h), 0)[1], 0)
        w_core = []
        for copies, span in ((w_two_l, left), (w_two_r, right)):
            for copy in copies:
                copy.wait_recv()
            part = wf.at[:, :, core, :, span]
            w_core.append(send(part, part, sibling))
        exchange(s_y, y, 3, 3)

        def across(h):
            cols = pl.ds(pl.multiple_of(h * DH, DH), DH)
            attn[:, cols] = (acc[:, cols] + dot(wqc[h], read[h // 2])).astype(BF16)

        lax.fori_loop(0, HEADS, lambda h, _: (across(h), 0)[1], 0)
        for copy in w_core:
            copy.wait_recv()

        def weights(block):
            return wf[block].reshape(WIDTH, WIDTH)

        def project(block):
            def step(t, _):
                span = pl.ds(pl.multiple_of(t * TILE, TILE), TILE)
                piece[block, span] = dot_nt(attn[span], weights(block)).astype(BF16)
                return 0

            lax.fori_loop(0, 2, step, 0)

        def z_half(block, part):
            return piece.at[block, pl.ds(part * TILE, TILE)]

        project(ring(z, 2))
        z_far = scatter_far(z_dev, z, z_half, zbuf)
        project(ring(z, 1))
        project(ring(z, -1))
        z_near = scatter_near(z_dev, z, z_half, zbuf)

        def back(block, start):
            def step(t, _):
                span = pl.ds(pl.multiple_of(t * TILE, TILE), TILE)
                term = dot(ogf[block, span], weights(block))
                acc[span] = term if start else acc[span] + term
                return 0

            lax.fori_loop(0, 2, step, 0)

        wg_core = []

        def weight_grad(block):
            def step(t, _):
                span = pl.ds(pl.multiple_of(t * TILE, TILE), TILE)
                term = dot_tn(ogf[block, :, span], attn[...]).astype(BF16)
                wg[block, pl.ds(t * 2, 2)] = term.reshape(2, 2, CH, WIDTH)
                return 0

            lax.fori_loop(0, 2, step, 0)
            wg_core.append(send(wg.at[block, :, 1 - core], wgc.at[block], sibling))

        back(z, True)
        weight_grad(z)
        project(z)
        og_copies[2].wait_recv()
        back(ring(z, -1), False)
        og_copies[3].wait_recv()
        back(ring(z, 1), False)
        weight_grad(ring(z, -1))
        weight_grad(ring(z, 1))
        og_far[0].wait_recv()
        og_far[1].wait_recv()
        back(ring(z, 2), False)
        ga[...] = acc[...].astype(BF16)
        weight_grad(ring(z, 2))

        def state_grad(g):
            value = jnp.zeros((DH, CROSS * DH), F32)
            for r in range(2):
                h = g * 2 + r
                cols = pl.ds(pl.multiple_of(h * DH, DH), DH)
                value += dot_tn(ga[:, cols], wqc[h])
            gmat[g] = value

        lax.fori_loop(0, GROUPS, lambda g, _: (state_grad(g), 0)[1], 0)

        def level_grad(number):
            return gmat[:, :, number * DH : (number + 1) * DH]

        g_y = []
        for o in (1, 2, 3):
            same = flag(y // 2 == ring(y, o) // 2)
            gsend[o] = (level_grad(3) * same + level_grad(4) * (1.0 - same)).astype(BF16)
            g_y.append(send(gsend.at[o], grecv.at[o], y_dev(o)))

        for copy in wg_core:
            copy.wait_recv()

        def merge(t, _):
            wgc[t] = (wg[t, :, core].astype(F32) + wgc[t].astype(F32)).astype(BF16)
            return 0

        lax.fori_loop(0, RING, merge, 0)
        wg_one_l = [
            send(wgc.at[ring(y, o), :, :, left], buf1.at[0, o], y_dev(o)) for o in (2, 1, 3)
        ]
        wg_one_r = [
            send(wgc.at[:, ring(x, o), :, right], buf1.at[1, o], x_dev(o)) for o in (2, 1, 3)
        ]

        def backward(g):
            group = pl.ds(pl.multiple_of(g * DH, DH), DH)
            k0, k1 = k_ref[first, group], k_ref[second, group]
            v0, v1 = v_ref[first, group], v_ref[second, group]
            for r in range(2):
                h = g * 2 + r
                cols = pl.ds(pl.multiple_of(h * DH, DH), DH)
                q0, q1 = q_ref[first, cols], q_ref[second, cols]
                g0, g1 = ga[first, cols], ga[second, cols]
                d0 = (dot_nt(g0, v0) * tile_weight(h, 0)).astype(BF16)
                d1 = (dot_nt(g1, v1) * tile_weight(h, 1)).astype(BF16)
                d2 = (dot_nt(g1, v0) * scale[h, second, 3:4]).astype(BF16)
                dq0 = dot(d0, k0)
                dq1 = dot(d1, k1) + dot(d2, k0)
                y0, y1 = dot_nt(g0, read[g]), dot_nt(g1, read[g])
                for l in range(CROSS):
                    part = slice(l * DH, (l + 1) * DH)
                    number = slice(LOCAL + l, LOCAL + l + 1)
                    dq0 += y0[:, part] * scale[h, first, number]
                    dq1 += y1[:, part] * scale[h, second, number]
                dq_ref[first, cols] = dq0.astype(BF16)
                dq_ref[second, cols] = dq1.astype(BF16)
                p0, p1, p2 = prob[h, 0], prob[h, 1], prob[h, 2]
                dk0 = dot_tn(d0, q0) + dot_tn(d2, q1)
                dk1 = dot_tn(d1, q1)
                dv0 = dot_tn(p0, g0) + dot_tn(p2, g1)
                dv1 = dot_tn(p1, g1)
                if r == 0:
                    dka[first, group] = dk0
                    dka[second, group] = dk1
                    dva[first, group] = dv0
                    dva[second, group] = dv1
                else:
                    dka[first, group] += dk0
                    dka[second, group] += dk1
                    dva[first, group] += dv0
                    dva[second, group] += dv1

        backward_loop = lambda a, b: lax.fori_loop(a, b, lambda g, _: (backward(g), 0)[1], 0)
        backward_loop(0, 1)
        z_middle = scatter_middle(z_dev, z, z_half, zbuf, z_far)
        gacc[...] = jnp.zeros_like(gacc)
        for o, copy in zip((1, 2, 3), g_y):
            copy.wait_recv()
            gacc[...] += grecv[o].astype(F32) * flag(ring(y, -o) > y)
        g_x = []
        for o in (1, 2, 3):
            same = flag(x // 2 == ring(x, o) // 2)
            lower = flag(x > ring(x, o))
            gsend[3 + o] = (
                gacc[...]
                + level_grad(1) * (lower * same)
                + level_grad(2) * (lower * (1.0 - same))
            ).astype(BF16)
            g_x.append(send(gsend.at[3 + o], grecv.at[3 + o], x_dev(o)))
        backward_loop(1, 2)
        for o, copy in zip((1, 2, 3), g_x):
            copy.wait_recv()
            gacc[...] += grecv[3 + o].astype(F32)
        gsend[0] = (gacc[...] + level_grad(0) * flag(core == 1)).astype(BF16)
        g_core = send(gsend.at[0], grecv.at[0], sibling)

        for copies, side, own in (
            (wg_one_l, 0, wgc[y, :, :, left]),
            (wg_one_r, 1, wgc[:, x, :, right]),
        ):
            for copy in copies:
                copy.wait_recv()
            value = own.astype(F32)
            for o in (1, 2, 3):
                value += buf1[side, o].astype(F32)
            half2[side] = value.astype(BF16)
        wg_two = [send(half2.at[0, ring(x, o)], buf2.at[0, o], x_dev(o)) for o in (2, 1, 3)]
        wg_two += [send(half2.at[1, ring(y, o)], buf2.at[1, o], y_dev(o)) for o in (2, 1, 3)]

        g_core.wait_recv()
        gacc[...] += grecv[0].astype(F32)
        for g in range(GROUPS):
            cols = slice(g * DH, (g + 1) * DH)
            key_side = gacc[g].astype(BF16)
            dk_ref[:, cols] = (dka[:, cols] + dot(v_ref[:, cols], key_side)).astype(BF16)
            dv_ref[:, cols] = (dva[:, cols] + dot_nt(k_ref[:, cols], key_side)).astype(BF16)

        for copy in wg_two:
            copy.wait_recv()
        for side, own, span in ((0, x, left), (1, y, right)):
            value = half2[side, own].astype(F32)
            for o in (1, 2, 3):
                value += buf2[side, o].astype(F32)
            wg_ref[:, span] = value * norm

        scatter_wait(z_near, z_middle)
        proj_ref[0:TILE] = scatter_sum(z, z_half, zbuf, 0).astype(BF16)
        proj_ref[TILE:] = scatter_sum(z, z_half, zbuf, 1).astype(BF16)
        for copy in sent:
            copy.wait_send()

    return kernel


COPIES = 64


def store(*refs):
    sem = refs[-1]
    copies = [
        pltpu.make_async_copy(refs[i], refs[5 + i], sem.at[i]) for i in range(5)
    ]
    for copy in copies:
        copy.start()
    for copy in copies:
        copy.wait()


def local(queries, key_heads, value_heads, class_ids, level_table, out_weight, out_grad):
    tokens = queries.shape[0]
    norm = (tokens * lax.axis_size("ctx")) ** (-0.5)
    levels = LOCAL + CROSS
    vmem = pl.BlockSpec(memory_space=pltpu.VMEM)
    scratch = [
        pltpu.VMEM((TOKENS, WIDTH), BF16),
        pltpu.VMEM((TOKENS, GROUPS * DH), BF16),
        pltpu.VMEM((TOKENS, GROUPS * DH), BF16),
        pltpu.VMEM((RING, TOKENS, WIDTH), BF16),
        pltpu.VMEM((RING, RING, 2, CH, WIDTH), BF16),
        pltpu.VMEM((TOKENS, WIDTH), F32),
        pltpu.VMEM((TOKENS, WIDTH), BF16),
        pltpu.VMEM((TOKENS, WIDTH), BF16),
        pltpu.VMEM((RING, TOKENS, WIDTH), BF16),
        pltpu.VMEM((6, TILE, WIDTH), BF16),
        pltpu.VMEM((RING, RING, 2, CH, WIDTH), BF16),
        pltpu.VMEM((RING, RING, CH, WIDTH), BF16),
        pltpu.VMEM((2, RING, RING, CH, TILE), BF16),
        pltpu.VMEM((2, RING, CH, TILE), BF16),
        pltpu.VMEM((2, RING, CH, TILE), BF16),
        pltpu.VMEM((HEADS, TOKENS, levels), F32),
        pltpu.VMEM((HEADS, TOKENS, CROSS * DH), BF16),
        pltpu.VMEM((HEADS, 3, TILE, TILE), BF16),
        pltpu.VMEM((GROUPS, DH, DH), F32),
        pltpu.VMEM((3, GROUPS, DH, DH), BF16),
        pltpu.VMEM((7, GROUPS, DH, DH), BF16),
        pltpu.VMEM((GROUPS, CROSS * DH, DH), BF16),
        pltpu.VMEM((GROUPS, DH, CROSS * DH), F32),
        pltpu.VMEM((GROUPS, DH, DH), F32),
        pltpu.VMEM((7, GROUPS, DH, DH), BF16),
        pltpu.VMEM((7, GROUPS, DH, DH), BF16),
        pltpu.VMEM((TOKENS, GROUPS * DH), F32),
        pltpu.VMEM((TOKENS, GROUPS * DH), F32),
        pltpu.SemaphoreType.DMA((5,)),
        pltpu.SemaphoreType.DMA((COPIES,)),
        pltpu.SemaphoreType.DMA((COPIES,)),
    ]
    hbm = pl.BlockSpec(memory_space=pl.ANY)
    shapes = (
        ((TOKENS, WIDTH), BF16),
        ((TOKENS, WIDTH), BF16),
        ((TOKENS, GROUPS * DH), BF16),
        ((TOKENS, GROUPS * DH), BF16),
        ((CH, WIDTH), F32),
    )
    results = pl.pallas_call(
        make_kernel(norm),
        out_shape=tuple(pltpu.VMEM(*shape) for shape in shapes),
        in_specs=[hbm, hbm, hbm, vmem, vmem, hbm, hbm],
        out_specs=(vmem,) * 5,
        scratch_shapes=scratch,
        compiler_params=pltpu.CompilerParams(
            collective_id=0, has_side_effects=True, vmem_limit_bytes=56 << 20
        ),
        name="layer",
    )(
        queries,
        key_heads,
        value_heads,
        class_ids.reshape(1, tokens),
        level_table.transpose(2, 1, 0),
        out_weight,
        out_grad,
    )
    return pl.pallas_call(
        store,
        out_shape=tuple(jax.ShapeDtypeStruct(*shape) for shape in shapes),
        in_specs=[vmem] * 5,
        out_specs=(pl.BlockSpec(memory_space=pl.ANY),) * 5,
        scratch_shapes=[pltpu.SemaphoreType.DMA((5,))],
        name="store",
    )(*(pltpu.with_memory_space_constraint(result, pltpu.VMEM) for result in results))


def solution(mesh):
    placed = (
        P("ctx", "heads"),
        P("ctx", "heads"),
        P("ctx", "heads"),
        P("ctx"),
        P(None, "heads", None),
        P("ctx", "heads"),
        P("ctx", "heads"),
    )
    return jax.shard_map(
        local,
        mesh=mesh,
        in_specs=placed,
        out_specs=(P("ctx", "heads"),) * 5,
        check_vma=False,
    )
```

```python
import jax
import jax.numpy as jnp
from jax import lax
from jax.experimental import pallas as pl
from jax.experimental.pallas import tpu as pltpu
from jax.sharding import PartitionSpec as P

DH = 128
CH = 64
RING = 4
LOCAL = 4
CROSS = 5
TILE = 256
TOKENS = 512
WIDTH = 512
HEADS = 4
GROUPS = 2
BF16 = jnp.bfloat16
F32 = jnp.float32


def coefficient(level):
    return DH ** (-0.5) * (CH * 2 ** max(level - 1, 0)) ** (-0.5)


def contract(a, b, da, db, precision=None):
    return lax.dot_general(
        a, b, (((da,), (db,)), ((), ())), preferred_element_type=F32, precision=precision
    )


def dot(a, b):
    return contract(a, b, 1, 0)


def dot_nt(a, b):
    return contract(a, b, 1, 1)


def dot_tn(a, b):
    return contract(a, b, 0, 0)


def ring(index, offset):
    return lax.rem(index + offset + RING, RING)


def flag(condition):
    return condition.astype(jnp.int32).astype(F32)


def make_kernel(norm):
    def kernel(
        q_hbm, k_hbm, v_hbm, ids_ref, tab_ref, w_hbm, og_hbm,
        proj_ref, dq_ref, dk_ref, dv_ref, wg_ref,
        q_ref, k_ref, v_ref, ogf, wf, acc, attn, ga, piece, zbuf, wg, wgc, buf1, half2, buf2,
        scale, wqc, prob, total, ssend, srecv, read, gmat, gacc, gsend, grecv, dka, dva,
        lsem, ssem, rsem,
    ):
        z = lax.axis_index("heads")
        c = lax.axis_index("ctx")
        core = lax.rem(c, 2)
        x = lax.rem(c // 2, RING)
        y = c // 8
        used = [0]
        sent = []

        def z_dev(offset):
            return {"heads": ring(z, offset)}

        def x_dev(offset):
            return {"ctx": (y * RING + ring(x, offset)) * 2 + core}

        def y_dev(offset):
            return {"ctx": (ring(y, offset) * RING + x) * 2 + core}

        sibling = {"ctx": (y * RING + x) * 2 + 1 - core}

        def send(src, dst, device):
            number = used[0]
            used[0] = number + 1
            copy = pltpu.make_async_remote_copy(
                src_ref=src,
                dst_ref=dst,
                send_sem=ssem.at[number],
                recv_sem=rsem.at[number],
                device_id=device,
                device_id_type=pl.DeviceIdType.MESH,
            )
            copy.start()
            sent.append(copy)
            return copy

        def gather_start(dev, index, half):
            right, left = dev(1), dev(-1)
            a = send(half(index, 0), half(index, 0), right)
            b = send(half(index, 1), half(index, 1), left)
            d = send(half(index, 1), half(index, 1), right)
            e = send(half(index, 0), half(index, 0), left)
            return a, b, d, e

        def gather_forward(dev, index, half, copies):
            before, after = ring(index, -1), ring(index, 1)
            copies[0].wait_recv()
            a = send(half(before, 0), half(before, 0), dev(1))
            copies[1].wait_recv()
            b = send(half(after, 1), half(after, 1), dev(-1))
            return a, b

        def scatter_far(dev, index, half, buf):
            far = ring(index, 2)
            return (
                send(half(far, 0), buf.at[0], dev(1)),
                send(half(far, 1), buf.at[3], dev(-1)),
            )

        def scatter_near(dev, index, half, buf):
            return (
                send(half(ring(index, 1), 1), buf.at[1], dev(1)),
                send(half(ring(index, -1), 0), buf.at[4], dev(-1)),
            )

        def scatter_middle(dev, index, half, buf, far):
            after, before = half(ring(index, 1), 0), half(ring(index, -1), 1)
            far[0].wait_recv()
            after[...] = (after[...].astype(F32) + buf[0].astype(F32)).astype(BF16)
            a = send(after, buf.at[2], dev(1))
            far[1].wait_recv()
            before[...] = (before[...].astype(F32) + buf[3].astype(F32)).astype(BF16)
            b = send(before, buf.at[5], dev(-1))
            return a, b

        def scatter_wait(near, middle):
            for copy in near + middle:
                copy.wait_recv()

        def scatter_sum(index, half, buf, part):
            own = half(index, part)[...].astype(F32)
            if part == 0:
                return own + buf[2].astype(F32) + buf[4].astype(F32)
            return own + buf[1].astype(F32) + buf[5].astype(F32)

        barrier = pltpu.get_barrier_semaphore()
        peers = [z_dev(1), z_dev(-1), sibling]
        for offset in (1, 2, 3):
            peers += [x_dev(offset), y_dev(offset)]
        for device in peers:
            pl.semaphore_signal(
                barrier, inc=1, device_id=device, device_id_type=pl.DeviceIdType.MESH
            )

        fetched = [
            pltpu.make_async_copy(source, target, lsem.at[i])
            for i, (source, target) in enumerate(
                (
                    (og_hbm, ogf.at[z]),
                    (w_hbm, wf.at[y, x, core]),
                    (k_hbm, k_ref),
                    (v_hbm, v_ref),
                    (q_hbm, q_ref),
                )
            )
        ]
        for copy in fetched:
            copy.start()
        for copy in fetched:
            copy.wait()
        pl.semaphore_wait(barrier, len(peers))

        def og_half(block, part):
            return ogf.at[block, pl.ds(part * TILE, TILE)]

        og_copies = gather_start(z_dev, z, og_half)

        left, right = pl.ds(0, TILE), pl.ds(TILE, TILE)
        mine_l = wf.at[y, x, core, :, left]
        mine_r = wf.at[y, x, core, :, right]
        w_one = [send(mine_l, mine_l, x_dev(o)) for o in (1, 3, 2)]
        w_one += [send(mine_r, mine_r, y_dev(o)) for o in (1, 3, 2)]

        for g in range(GROUPS):
            cols = slice(g * DH, (g + 1) * DH)
            total[g] = dot_tn(k_ref[:, cols], v_ref[:, cols])
        ssend[0] = total[...].astype(BF16)
        s_core = send(ssend.at[0], srecv.at[0], sibling)

        classes = tab_ref.shape[2]
        onehot = (
            lax.broadcasted_iota(jnp.int32, (classes, TOKENS), 0) == ids_ref[...]
        ).astype(F32)
        levels = LOCAL + CROSS
        level = lax.broadcasted_iota(jnp.int32, (1, levels), 1)
        coef = jnp.full((1, levels), coefficient(0), F32)
        for number in range(1, levels):
            coef = jnp.where(level == number, coefficient(number), coef)
        for h in range(HEADS):
            lam = contract(onehot, tab_ref[:, h, :], 0, 1, lax.Precision.HIGHEST)
            scale[h] = lam * coef

        s_core.wait_recv()
        got = srecv[0].astype(F32)
        for g in range(GROUPS):
            read[g, 0:DH] = (got[g] * flag(core == 1)).astype(BF16)
        total[...] += got
        ssend[1] = total[...].astype(BF16)
        s_x = [send(ssend.at[1], srecv.at[o], x_dev(o)) for o in (1, 2, 3)]

        for copy in w_one:
            copy.wait_recv()
        row_l = wf.at[y, :, core, :, left]
        row_r = wf.at[:, x, core, :, right]
        w_two_l = [send(row_l, row_l, y_dev(o)) for o in (1, 3, 2)]
        w_two_r = [send(row_r, row_r, x_dev(o)) for o in (1, 3, 2)]

        def weigh(h):
            cols = pl.ds(pl.multiple_of(h * DH, DH), DH)
            q = q_ref[:, cols].astype(F32)
            for l in range(CROSS):
                wqc[h, :, l * DH : (l + 1) * DH] = (
                    q * scale[h, :, LOCAL + l : LOCAL + l + 1]
                ).astype(BF16)

        lax.fori_loop(0, HEADS, lambda h, _: (weigh(h), 0)[1], 0)

        og_far = gather_forward(z_dev, z, og_half, og_copies)

        def exchange(copies, position, slot, low):
            near = jnp.zeros((GROUPS, DH, DH), F32)
            far = jnp.zeros((GROUPS, DH, DH), F32)
            everything = total[...]
            for o, copy in zip((1, 2, 3), copies):
                copy.wait_recv()
                source = ring(position, -o)
                value = srecv[slot + o].astype(F32)
                upper = source < position
                same = source // 2 == position // 2
                near += value * flag(jnp.logical_and(upper, same))
                far += value * flag(jnp.logical_and(upper, jnp.logical_not(same)))
                everything += value
            for g in range(GROUPS):
                read[g, low * DH : (low + 1) * DH] = near[g].astype(BF16)
                read[g, (low + 1) * DH : (low + 2) * DH] = far[g].astype(BF16)
            total[...] = everything

        exchange(s_x, x, 0, 1)
        ssend[2] = total[...].astype(BF16)
        s_y = [send(ssend.at[2], srecv.at[3 + o], y_dev(o)) for o in (1, 2, 3)]

        rows = lax.broadcasted_iota(jnp.int32, (TILE, TILE), 0)
        cols_ = lax.broadcasted_iota(jnp.int32, (TILE, TILE), 1)

        def tile_weight(h, i):
            span = pl.ds(i * TILE, TILE)
            weight = jnp.where(
                rows // (2 * CH) > cols_ // (2 * CH), scale[h, span, 2:3], 0.0
            )
            weight = jnp.where(
                jnp.logical_and(
                    rows // (2 * CH) == cols_ // (2 * CH), rows // CH > cols_ // CH
                ),
                scale[h, span, 1:2],
                weight,
            )
            return jnp.where(
                jnp.logical_and(rows // CH == cols_ // CH, rows >= cols_),
                scale[h, span, 0:1],
                weight,
            )

        first, second = pl.ds(0, TILE), pl.ds(TILE, TILE)

        def forward(h):
            cols = pl.ds(pl.multiple_of(h * DH, DH), DH)
            group = pl.ds(pl.multiple_of(h // 2 * DH, DH), DH)
            q0, q1 = q_ref[first, cols], q_ref[second, cols]
            k0, k1 = k_ref[first, group], k_ref[second, group]
            v0, v1 = v_ref[first, group], v_ref[second, group]
            p0 = (dot_nt(q0, k0) * tile_weight(h, 0)).astype(BF16)
            p1 = (dot_nt(q1, k1) * tile_weight(h, 1)).astype(BF16)
            p2 = (dot_nt(q1, k0) * scale[h, second, 3:4]).astype(BF16)
            prob[h, 0] = p0
            prob[h, 1] = p1
            prob[h, 2] = p2
            acc[first, cols] = dot(p0, v0)
            acc[second, cols] = dot(p1, v1) + dot(p2, v0)

        lax.fori_loop(0, HEADS, lambda h, _: (forward(h), 0)[1], 0)
        w_core = []
        for copies, span in ((w_two_l, left), (w_two_r, right)):
            for copy in copies:
                copy.wait_recv()
            part = wf.at[:, :, core, :, span]
            w_core.append(send(part, part, sibling))
        exchange(s_y, y, 3, 3)

        def across(h):
            cols = pl.ds(pl.multiple_of(h * DH, DH), DH)
            attn[:, cols] = (acc[:, cols] + dot(wqc[h], read[h // 2])).astype(BF16)

        lax.fori_loop(0, HEADS, lambda h, _: (across(h), 0)[1], 0)
        for copy in w_core:
            copy.wait_recv()

        def weights(block):
            return wf[block].reshape(WIDTH, WIDTH)

        def project(block):
            piece[block] = dot_nt(attn[...], weights(block)).astype(BF16)

        def z_half(block, part):
            return piece.at[block, pl.ds(part * TILE, TILE)]

        def back(block):
            return dot(ogf[block], weights(block))

        wg_core = []

        def weight_grad(block):
            term = dot_tn(ogf[block], attn[...]).astype(BF16)
            wg[block] = term.reshape(RING, 2, CH, WIDTH)
            wg_core.append(send(wg.at[block, :, 1 - core], wgc.at[block], sibling))

        project(ring(z, 2))
        z_far = scatter_far(z_dev, z, z_half, zbuf)
        og_copies[2].wait_recv()
        og_copies[3].wait_recv()
        acc[...] = back(z) + back(ring(z, -1)) + back(ring(z, 1))
        project(ring(z, 1))
        project(ring(z, -1))
        z_near = scatter_near(z_dev, z, z_half, zbuf)
        weight_grad(z)
        weight_grad(ring(z, -1))
        weight_grad(ring(z, 1))
        og_far[0].wait_recv()
        og_far[1].wait_recv()
        ga[...] = (acc[...] + back(ring(z, 2))).astype(BF16)

        def state_grad(g):
            value = jnp.zeros((DH, CROSS * DH), F32)
            for r in range(2):
                h = g * 2 + r
                cols = pl.ds(pl.multiple_of(h * DH, DH), DH)
                value += dot_tn(ga[:, cols], wqc[h])
            gmat[g] = value

        lax.fori_loop(0, GROUPS, lambda g, _: (state_grad(g), 0)[1], 0)

        def level_grad(number):
            return gmat[:, :, number * DH : (number + 1) * DH]

        g_y = []
        for o in (1, 2, 3):
            same = flag(y // 2 == ring(y, o) // 2)
            gsend[o] = (level_grad(3) * same + level_grad(4) * (1.0 - same)).astype(BF16)
            g_y.append(send(gsend.at[o], grecv.at[o], y_dev(o)))

        weight_grad(ring(z, 2))
        project(z)
        for copy in wg_core:
            copy.wait_recv()

        def merge(t, _):
            wgc[t] = (wg[t, :, core].astype(F32) + wgc[t].astype(F32)).astype(BF16)
            return 0

        lax.fori_loop(0, RING, merge, 0)
        gacc[...] = jnp.zeros_like(gacc)
        for o, copy in zip((1, 2, 3), g_y):
            copy.wait_recv()
            gacc[...] += grecv[o].astype(F32) * flag(ring(y, -o) > y)
        g_x = []
        for o in (1, 2, 3):
            same = flag(x // 2 == ring(x, o) // 2)
            lower = flag(x > ring(x, o))
            gsend[3 + o] = (
                gacc[...]
                + level_grad(1) * (lower * same)
                + level_grad(2) * (lower * (1.0 - same))
            ).astype(BF16)
            g_x.append(send(gsend.at[3 + o], grecv.at[3 + o], x_dev(o)))
        wg_one_l = [
            send(wgc.at[ring(y, o), :, :, left], buf1.at[0, o], y_dev(o)) for o in (2, 1, 3)
        ]
        wg_one_r = [
            send(wgc.at[:, ring(x, o), :, right], buf1.at[1, o], x_dev(o)) for o in (2, 1, 3)
        ]

        def backward(g):
            group = pl.ds(pl.multiple_of(g * DH, DH), DH)
            k0, k1 = k_ref[first, group], k_ref[second, group]
            v0, v1 = v_ref[first, group], v_ref[second, group]
            for r in range(2):
                h = g * 2 + r
                cols = pl.ds(pl.multiple_of(h * DH, DH), DH)
                q0, q1 = q_ref[first, cols], q_ref[second, cols]
                g0, g1 = ga[first, cols], ga[second, cols]
                d0 = (dot_nt(g0, v0) * tile_weight(h, 0)).astype(BF16)
                d1 = (dot_nt(g1, v1) * tile_weight(h, 1)).astype(BF16)
                d2 = (dot_nt(g1, v0) * scale[h, second, 3:4]).astype(BF16)
                dq0 = dot(d0, k0)
                dq1 = dot(d1, k1) + dot(d2, k0)
                y0, y1 = dot_nt(g0, read[g]), dot_nt(g1, read[g])
                for l in range(CROSS):
                    part = slice(l * DH, (l + 1) * DH)
                    number = slice(LOCAL + l, LOCAL + l + 1)
                    dq0 += y0[:, part] * scale[h, first, number]
                    dq1 += y1[:, part] * scale[h, second, number]
                dq_ref[first, cols] = dq0.astype(BF16)
                dq_ref[second, cols] = dq1.astype(BF16)
                p0, p1, p2 = prob[h, 0], prob[h, 1], prob[h, 2]
                dk0 = dot_tn(d0, q0) + dot_tn(d2, q1)
                dk1 = dot_tn(d1, q1)
                dv0 = dot_tn(p0, g0) + dot_tn(p2, g1)
                dv1 = dot_tn(p1, g1)
                if r == 0:
                    dka[first, group] = dk0
                    dka[second, group] = dk1
                    dva[first, group] = dv0
                    dva[second, group] = dv1
                else:
                    dka[first, group] += dk0
                    dka[second, group] += dk1
                    dva[first, group] += dv0
                    dva[second, group] += dv1

        backward_loop = lambda a, b: lax.fori_loop(a, b, lambda g, _: (backward(g), 0)[1], 0)
        backward_loop(0, 1)
        z_middle = scatter_middle(z_dev, z, z_half, zbuf, z_far)
        backward_loop(1, 2)
        for o, copy in zip((1, 2, 3), g_x):
            copy.wait_recv()
            gacc[...] += grecv[3 + o].astype(F32)
        gsend[0] = (gacc[...] + level_grad(0) * flag(core == 1)).astype(BF16)
        g_core = send(gsend.at[0], grecv.at[0], sibling)

        for copies, side, own in (
            (wg_one_l, 0, wgc[y, :, :, left]),
            (wg_one_r, 1, wgc[:, x, :, right]),
        ):
            for copy in copies:
                copy.wait_recv()
            value = own.astype(F32)
            for o in (1, 2, 3):
                value += buf1[side, o].astype(F32)
            half2[side] = value.astype(BF16)
        wg_two = [send(half2.at[0, ring(x, o)], buf2.at[0, o], x_dev(o)) for o in (2, 1, 3)]
        wg_two += [send(half2.at[1, ring(y, o)], buf2.at[1, o], y_dev(o)) for o in (2, 1, 3)]

        g_core.wait_recv()
        gacc[...] += grecv[0].astype(F32)
        for g in range(GROUPS):
            cols = slice(g * DH, (g + 1) * DH)
            key_side = gacc[g].astype(BF16)
            dk_ref[:, cols] = (dka[:, cols] + dot(v_ref[:, cols], key_side)).astype(BF16)
            dv_ref[:, cols] = (dva[:, cols] + dot_nt(k_ref[:, cols], key_side)).astype(BF16)

        for copy in wg_two:
            copy.wait_recv()
        for side, own, span in ((0, x, left), (1, y, right)):
            value = half2[side, own].astype(F32)
            for o in (1, 2, 3):
                value += buf2[side, o].astype(F32)
            wg_ref[:, span] = value * norm

        scatter_wait(z_near, z_middle)
        proj_ref[0:TILE] = scatter_sum(z, z_half, zbuf, 0).astype(BF16)
        proj_ref[TILE:] = scatter_sum(z, z_half, zbuf, 1).astype(BF16)
        for copy in sent:
            copy.wait_send()

    return kernel


COPIES = 64


def store(*refs):
    sem = refs[-1]
    copies = [
        pltpu.make_async_copy(refs[i], refs[5 + i], sem.at[i]) for i in range(5)
    ]
    for copy in copies:
        copy.start()
    for copy in copies:
        copy.wait()


def local(queries, key_heads, value_heads, class_ids, level_table, out_weight, out_grad):
    tokens = queries.shape[0]
    norm = (tokens * lax.axis_size("ctx")) ** (-0.5)
    levels = LOCAL + CROSS
    vmem = pl.BlockSpec(memory_space=pltpu.VMEM)
    scratch = [
        pltpu.VMEM((TOKENS, WIDTH), BF16),
        pltpu.VMEM((TOKENS, GROUPS * DH), BF16),
        pltpu.VMEM((TOKENS, GROUPS * DH), BF16),
        pltpu.VMEM((RING, TOKENS, WIDTH), BF16),
        pltpu.VMEM((RING, RING, 2, CH, WIDTH), BF16),
        pltpu.VMEM((TOKENS, WIDTH), F32),
        pltpu.VMEM((TOKENS, WIDTH), BF16),
        pltpu.VMEM((TOKENS, WIDTH), BF16),
        pltpu.VMEM((RING, TOKENS, WIDTH), BF16),
        pltpu.VMEM((6, TILE, WIDTH), BF16),
        pltpu.VMEM((RING, RING, 2, CH, WIDTH), BF16),
        pltpu.VMEM((RING, RING, CH, WIDTH), BF16),
        pltpu.VMEM((2, RING, RING, CH, TILE), BF16),
        pltpu.VMEM((2, RING, CH, TILE), BF16),
        pltpu.VMEM((2, RING, CH, TILE), BF16),
        pltpu.VMEM((HEADS, TOKENS, levels), F32),
        pltpu.VMEM((HEADS, TOKENS, CROSS * DH), BF16),
        pltpu.VMEM((HEADS, 3, TILE, TILE), BF16),
        pltpu.VMEM((GROUPS, DH, DH), F32),
        pltpu.VMEM((3, GROUPS, DH, DH), BF16),
        pltpu.VMEM((7, GROUPS, DH, DH), BF16),
        pltpu.VMEM((GROUPS, CROSS * DH, DH), BF16),
        pltpu.VMEM((GROUPS, DH, CROSS * DH), F32),
        pltpu.VMEM((GROUPS, DH, DH), F32),
        pltpu.VMEM((7, GROUPS, DH, DH), BF16),
        pltpu.VMEM((7, GROUPS, DH, DH), BF16),
        pltpu.VMEM((TOKENS, GROUPS * DH), F32),
        pltpu.VMEM((TOKENS, GROUPS * DH), F32),
        pltpu.SemaphoreType.DMA((5,)),
        pltpu.SemaphoreType.DMA((COPIES,)),
        pltpu.SemaphoreType.DMA((COPIES,)),
    ]
    hbm = pl.BlockSpec(memory_space=pl.ANY)
    shapes = (
        ((TOKENS, WIDTH), BF16),
        ((TOKENS, WIDTH), BF16),
        ((TOKENS, GROUPS * DH), BF16),
        ((TOKENS, GROUPS * DH), BF16),
        ((CH, WIDTH), F32),
    )
    results = pl.pallas_call(
        make_kernel(norm),
        out_shape=tuple(pltpu.VMEM(*shape) for shape in shapes),
        in_specs=[hbm, hbm, hbm, vmem, vmem, hbm, hbm],
        out_specs=(vmem,) * 5,
        scratch_shapes=scratch,
        compiler_params=pltpu.CompilerParams(
            collective_id=0, has_side_effects=True, vmem_limit_bytes=56 << 20
        ),
        name="layer",
    )(
        queries,
        key_heads,
        value_heads,
        class_ids.reshape(1, tokens),
        level_table.transpose(2, 1, 0),
        out_weight,
        out_grad,
    )
    return pl.pallas_call(
        store,
        out_shape=tuple(jax.ShapeDtypeStruct(*shape) for shape in shapes),
        in_specs=[vmem] * 5,
        out_specs=(pl.BlockSpec(memory_space=pl.ANY),) * 5,
        scratch_shapes=[pltpu.SemaphoreType.DMA((5,))],
        name="store",
    )(*(pltpu.with_memory_space_constraint(result, pltpu.VMEM) for result in results))


def solution(mesh):
    placed = (
        P("ctx", "heads"),
        P("ctx", "heads"),
        P("ctx", "heads"),
        P("ctx"),
        P(None, "heads", None),
        P("ctx", "heads"),
        P("ctx", "heads"),
    )
    return jax.shard_map(
        local,
        mesh=mesh,
        in_specs=placed,
        out_specs=(P("ctx", "heads"),) * 5,
        check_vma=False,
    )
```

```python
import jax
import jax.numpy as jnp
from jax import lax
from jax.experimental import pallas as pl
from jax.experimental.pallas import tpu as pltpu
from jax.sharding import PartitionSpec as P

DH = 128
CH = 64
RING = 4
LOCAL = 4
CROSS = 5
TILE = 256
TOKENS = 512
WIDTH = 512
HEADS = 4
GROUPS = 2
BF16 = jnp.bfloat16
F32 = jnp.float32


def coefficient(level):
    return DH ** (-0.5) * (CH * 2 ** max(level - 1, 0)) ** (-0.5)


def contract(a, b, da, db, precision=None):
    return lax.dot_general(
        a, b, (((da,), (db,)), ((), ())), preferred_element_type=F32, precision=precision
    )


def dot(a, b):
    return contract(a, b, 1, 0)


def dot_nt(a, b):
    return contract(a, b, 1, 1)


def dot_tn(a, b):
    return contract(a, b, 0, 0)


def ring(index, offset):
    return lax.rem(index + offset + RING, RING)


def flag(condition):
    return condition.astype(jnp.int32).astype(F32)


def make_kernel(norm):
    def kernel(
        q_hbm, k_hbm, v_hbm, ids_hbm, tab_hbm, w_hbm, og_hbm,
        proj_ref, dq_ref, dk_ref, dv_ref, wg_ref,
        q_ref, k_ref, v_ref, ids_ref, tab_ref, ogf, wf, acc, attn, ga, piece, zbuf, wg, wgc, buf1, half2, buf2,
        scale, wqc, prob, total, ssend, srecv, read, gmat, gacc, gsend, grecv, dka, dva,
        lsem, ssem, rsem,
    ):
        z = lax.axis_index("heads")
        c = lax.axis_index("ctx")
        core = lax.rem(c, 2)
        x = lax.rem(c // 2, RING)
        y = c // 8
        used = [0]
        sent = []

        def z_dev(offset):
            return {"heads": ring(z, offset)}

        def x_dev(offset):
            return {"ctx": (y * RING + ring(x, offset)) * 2 + core}

        def y_dev(offset):
            return {"ctx": (ring(y, offset) * RING + x) * 2 + core}

        sibling = {"ctx": (y * RING + x) * 2 + 1 - core}

        def send(src, dst, device):
            number = used[0]
            used[0] = number + 1
            copy = pltpu.make_async_remote_copy(
                src_ref=src,
                dst_ref=dst,
                send_sem=ssem.at[number],
                recv_sem=rsem.at[number],
                device_id=device,
                device_id_type=pl.DeviceIdType.MESH,
            )
            copy.start()
            sent.append(copy)
            return copy

        def gather_start(dev, index, source, half):
            right, left = dev(1), dev(-1)
            a = send(source(0), half(index, 0), right)
            b = send(source(1), half(index, 1), left)
            d = send(source(1), half(index, 1), right)
            e = send(source(0), half(index, 0), left)
            return a, b, d, e

        def gather_forward(dev, index, half, copies):
            before, after = ring(index, -1), ring(index, 1)
            copies[0].wait_recv()
            a = send(half(before, 0), half(before, 0), dev(1))
            copies[1].wait_recv()
            b = send(half(after, 1), half(after, 1), dev(-1))
            return a, b

        def scatter_far(dev, index, half, buf):
            far = ring(index, 2)
            return (
                send(half(far, 0), buf.at[0], dev(1)),
                send(half(far, 1), buf.at[3], dev(-1)),
            )

        def scatter_near(dev, index, half, buf):
            return (
                send(half(ring(index, 1), 1), buf.at[1], dev(1)),
                send(half(ring(index, -1), 0), buf.at[4], dev(-1)),
            )

        def scatter_middle(dev, index, half, buf, far):
            after, before = half(ring(index, 1), 0), half(ring(index, -1), 1)
            far[0].wait_recv()
            after[...] = (after[...].astype(F32) + buf[0].astype(F32)).astype(BF16)
            a = send(after, buf.at[2], dev(1))
            far[1].wait_recv()
            before[...] = (before[...].astype(F32) + buf[3].astype(F32)).astype(BF16)
            b = send(before, buf.at[5], dev(-1))
            return a, b

        barrier = pltpu.get_barrier_semaphore()
        peers = [z_dev(1), z_dev(-1), sibling]
        for offset in (1, 2, 3):
            peers += [x_dev(offset), y_dev(offset)]
        for device in peers:
            pl.semaphore_signal(
                barrier, inc=1, device_id=device, device_id_type=pl.DeviceIdType.MESH
            )

        fetched = [
            pltpu.make_async_copy(source, target, lsem.at[i])
            for i, (source, target) in enumerate(
                (
                    (og_hbm, ogf.at[z]),
                    (w_hbm, wf.at[y, x, core]),
                    (k_hbm, k_ref),
                    (v_hbm, v_ref),
                    (q_hbm, q_ref),
                    (ids_hbm, ids_ref),
                    (tab_hbm, tab_ref),
                )
            )
        ]
        for copy in fetched:
            copy.start()
        pl.semaphore_wait(barrier, len(peers))

        def og_half(block, part):
            return ogf.at[block, pl.ds(part * TILE, TILE)]

        def og_own(part):
            return og_hbm.at[pl.ds(part * TILE, TILE)]

        og_copies = gather_start(z_dev, z, og_own, og_half)

        left, right = pl.ds(0, TILE), pl.ds(TILE, TILE)
        mine_l = wf.at[y, x, core, :, left]
        mine_r = wf.at[y, x, core, :, right]
        w_one = [send(w_hbm.at[:, left], mine_l, x_dev(o)) for o in (1, 3, 2)]
        w_one += [send(w_hbm.at[:, right], mine_r, y_dev(o)) for o in (1, 3, 2)]

        fetched[2].wait()
        fetched[3].wait()
        for g in range(GROUPS):
            cols = slice(g * DH, (g + 1) * DH)
            total[g] = dot_tn(k_ref[:, cols], v_ref[:, cols])
        ssend[0] = total[...].astype(BF16)
        s_core = send(ssend.at[0], srecv.at[0], sibling)

        for copy in fetched[4:] + fetched[:2]:
            copy.wait()
        classes = tab_ref.shape[2]
        onehot = (
            lax.broadcasted_iota(jnp.int32, (classes, TOKENS), 0) == ids_ref[...]
        ).astype(F32)
        levels = LOCAL + CROSS
        level = lax.broadcasted_iota(jnp.int32, (1, levels), 1)
        coef = jnp.full((1, levels), coefficient(0), F32)
        for number in range(1, levels):
            coef = jnp.where(level == number, coefficient(number), coef)
        for h in range(HEADS):
            lam = contract(onehot, tab_ref[:, h, :], 0, 1, lax.Precision.HIGHEST)
            scale[h] = lam * coef

        s_core.wait_recv()
        got = srecv[0].astype(F32)
        for g in range(GROUPS):
            read[g, 0:DH] = (got[g] * flag(core == 1)).astype(BF16)
        total[...] += got
        ssend[1] = total[...].astype(BF16)
        s_x = [send(ssend.at[1], srecv.at[o], x_dev(o)) for o in (1, 2, 3)]

        for copy in w_one:
            copy.wait_recv()
        row_l = wf.at[y, :, core, :, left]
        row_r = wf.at[:, x, core, :, right]
        w_two_l = [send(row_l, row_l, y_dev(o)) for o in (1, 3, 2)]
        w_two_r = [send(row_r, row_r, x_dev(o)) for o in (1, 3, 2)]

        def weigh(h):
            cols = pl.ds(pl.multiple_of(h * DH, DH), DH)
            q = q_ref[:, cols].astype(F32)
            for l in range(CROSS):
                wqc[h, :, l * DH : (l + 1) * DH] = (
                    q * scale[h, :, LOCAL + l : LOCAL + l + 1]
                ).astype(BF16)

        lax.fori_loop(0, HEADS, lambda h, _: (weigh(h), 0)[1], 0)

        og_far = gather_forward(z_dev, z, og_half, og_copies)

        def exchange(copies, position, slot, low):
            near = jnp.zeros((GROUPS, DH, DH), F32)
            far = jnp.zeros((GROUPS, DH, DH), F32)
            everything = total[...]
            for o, copy in zip((1, 2, 3), copies):
                copy.wait_recv()
                source = ring(position, -o)
                value = srecv[slot + o].astype(F32)
                upper = source < position
                same = source // 2 == position // 2
                near += value * flag(jnp.logical_and(upper, same))
                far += value * flag(jnp.logical_and(upper, jnp.logical_not(same)))
                everything += value
            for g in range(GROUPS):
                read[g, low * DH : (low + 1) * DH] = near[g].astype(BF16)
                read[g, (low + 1) * DH : (low + 2) * DH] = far[g].astype(BF16)
            total[...] = everything

        exchange(s_x, x, 0, 1)
        ssend[2] = total[...].astype(BF16)
        s_y = [send(ssend.at[2], srecv.at[3 + o], y_dev(o)) for o in (1, 2, 3)]

        rows = lax.broadcasted_iota(jnp.int32, (TILE, TILE), 0)
        cols_ = lax.broadcasted_iota(jnp.int32, (TILE, TILE), 1)

        def tile_weight(h, i):
            span = pl.ds(i * TILE, TILE)
            weight = jnp.where(
                rows // (2 * CH) > cols_ // (2 * CH), scale[h, span, 2:3], 0.0
            )
            weight = jnp.where(
                jnp.logical_and(
                    rows // (2 * CH) == cols_ // (2 * CH), rows // CH > cols_ // CH
                ),
                scale[h, span, 1:2],
                weight,
            )
            return jnp.where(
                jnp.logical_and(rows // CH == cols_ // CH, rows >= cols_),
                scale[h, span, 0:1],
                weight,
            )

        first, second = pl.ds(0, TILE), pl.ds(TILE, TILE)

        def forward(h):
            cols = pl.ds(pl.multiple_of(h * DH, DH), DH)
            group = pl.ds(pl.multiple_of(h // 2 * DH, DH), DH)
            q0, q1 = q_ref[first, cols], q_ref[second, cols]
            k0, k1 = k_ref[first, group], k_ref[second, group]
            v0, v1 = v_ref[first, group], v_ref[second, group]
            p0 = (dot_nt(q0, k0) * tile_weight(h, 0)).astype(BF16)
            p1 = (dot_nt(q1, k1) * tile_weight(h, 1)).astype(BF16)
            p2 = (dot_nt(q1, k0) * scale[h, second, 3:4]).astype(BF16)
            prob[h, 0] = p0
            prob[h, 1] = p1
            prob[h, 2] = p2
            acc[first, cols] = dot(p0, v0)
            acc[second, cols] = dot(p1, v1) + dot(p2, v0)

        lax.fori_loop(0, HEADS, lambda h, _: (forward(h), 0)[1], 0)
        w_core = []
        for copies, span in ((w_two_l, left), (w_two_r, right)):
            for copy in copies:
                copy.wait_recv()
            part = wf.at[:, :, core, :, span]
            w_core.append(send(part, part, sibling))
        exchange(s_y, y, 3, 3)

        def across(h):
            cols = pl.ds(pl.multiple_of(h * DH, DH), DH)
            attn[:, cols] = (acc[:, cols] + dot(wqc[h], read[h // 2])).astype(BF16)

        lax.fori_loop(0, HEADS, lambda h, _: (across(h), 0)[1], 0)
        for copy in w_core:
            copy.wait_recv()

        def weights(block):
            return wf[block].reshape(WIDTH, WIDTH)

        def project(block):
            piece[block] = dot_nt(attn[...], weights(block)).astype(BF16)

        def z_half(block, part):
            return piece.at[block, pl.ds(part * TILE, TILE)]

        def back(block):
            return dot(ogf[block], weights(block))

        wg_core = []

        def weight_grad(block):
            term = dot_tn(ogf[block], attn[...]).astype(BF16)
            wg[block] = term.reshape(RING, 2, CH, WIDTH)
            wg_core.append(send(wg.at[block, :, 1 - core], wgc.at[block], sibling))

        project(ring(z, 2))
        z_far = scatter_far(z_dev, z, z_half, zbuf)
        og_copies[2].wait_recv()
        og_copies[3].wait_recv()
        acc[...] = back(z) + back(ring(z, -1)) + back(ring(z, 1))
        project(ring(z, 1))
        project(ring(z, -1))
        z_near = scatter_near(z_dev, z, z_half, zbuf)
        weight_grad(z)
        weight_grad(ring(z, -1))
        weight_grad(ring(z, 1))
        og_far[0].wait_recv()
        og_far[1].wait_recv()
        ga[...] = (acc[...] + back(ring(z, 2))).astype(BF16)
        weight_grad(ring(z, 2))

        def state_grad(g):
            value = jnp.zeros((DH, CROSS * DH), F32)
            for r in range(2):
                h = g * 2 + r
                cols = pl.ds(pl.multiple_of(h * DH, DH), DH)
                value += dot_tn(ga[:, cols], wqc[h])
            gmat[g] = value

        lax.fori_loop(0, GROUPS, lambda g, _: (state_grad(g), 0)[1], 0)

        def level_grad(number):
            return gmat[:, :, number * DH : (number + 1) * DH]

        g_y = []
        for o in (1, 2, 3):
            same = flag(y // 2 == ring(y, o) // 2)
            gsend[o] = (level_grad(3) * same + level_grad(4) * (1.0 - same)).astype(BF16)
            g_y.append(send(gsend.at[o], grecv.at[o], y_dev(o)))

        for copy in wg_core:
            copy.wait_recv()

        def merge(t, _):
            wgc[t] = (wg[t, :, core].astype(F32) + wgc[t].astype(F32)).astype(BF16)
            return 0

        lax.fori_loop(0, RING, merge, 0)
        wg_one_l = [
            send(wgc.at[ring(y, o), :, :, left], buf1.at[0, o], y_dev(o)) for o in (2, 1, 3)
        ]
        project(z)
        gacc[...] = jnp.zeros_like(gacc)
        for o, copy in zip((1, 2, 3), g_y):
            copy.wait_recv()
            gacc[...] += grecv[o].astype(F32) * flag(ring(y, -o) > y)
        g_x = []
        for o in (1, 2, 3):
            same = flag(x // 2 == ring(x, o) // 2)
            lower = flag(x > ring(x, o))
            gsend[3 + o] = (
                gacc[...]
                + level_grad(1) * (lower * same)
                + level_grad(2) * (lower * (1.0 - same))
            ).astype(BF16)
            g_x.append(send(gsend.at[3 + o], grecv.at[3 + o], x_dev(o)))
        wg_one_r = [
            send(wgc.at[:, ring(x, o), :, right], buf1.at[1, o], x_dev(o)) for o in (2, 1, 3)
        ]

        def backward(g):
            group = pl.ds(pl.multiple_of(g * DH, DH), DH)
            k0, k1 = k_ref[first, group], k_ref[second, group]
            v0, v1 = v_ref[first, group], v_ref[second, group]
            for r in range(2):
                h = g * 2 + r
                cols = pl.ds(pl.multiple_of(h * DH, DH), DH)
                q0, q1 = q_ref[first, cols], q_ref[second, cols]
                g0, g1 = ga[first, cols], ga[second, cols]
                d0 = (dot_nt(g0, v0) * tile_weight(h, 0)).astype(BF16)
                d1 = (dot_nt(g1, v1) * tile_weight(h, 1)).astype(BF16)
                d2 = (dot_nt(g1, v0) * scale[h, second, 3:4]).astype(BF16)
                dq0 = dot(d0, k0)
                dq1 = dot(d1, k1) + dot(d2, k0)
                y0, y1 = dot_nt(g0, read[g]), dot_nt(g1, read[g])
                for l in range(CROSS):
                    part = slice(l * DH, (l + 1) * DH)
                    number = slice(LOCAL + l, LOCAL + l + 1)
                    dq0 += y0[:, part] * scale[h, first, number]
                    dq1 += y1[:, part] * scale[h, second, number]
                dq_ref[first, cols] = dq0.astype(BF16)
                dq_ref[second, cols] = dq1.astype(BF16)
                p0, p1, p2 = prob[h, 0], prob[h, 1], prob[h, 2]
                dk0 = dot_tn(d0, q0) + dot_tn(d2, q1)
                dk1 = dot_tn(d1, q1)
                dv0 = dot_tn(p0, g0) + dot_tn(p2, g1)
                dv1 = dot_tn(p1, g1)
                if r == 0:
                    dka[first, group] = dk0
                    dka[second, group] = dk1
                    dva[first, group] = dv0
                    dva[second, group] = dv1
                else:
                    dka[first, group] += dk0
                    dka[second, group] += dk1
                    dva[first, group] += dv0
                    dva[second, group] += dv1

        backward_loop = lambda a, b: lax.fori_loop(a, b, lambda g, _: (backward(g), 0)[1], 0)
        z_middle = scatter_middle(z_dev, z, z_half, zbuf, z_far)
        backward_loop(0, 1)
        for o, copy in zip((1, 2, 3), g_x):
            copy.wait_recv()
            gacc[...] += grecv[3 + o].astype(F32)
        gsend[0] = (gacc[...] + level_grad(0) * flag(core == 1)).astype(BF16)
        g_core = send(gsend.at[0], grecv.at[0], sibling)
        backward_loop(1, 2)

        for copies, side, own in (
            (wg_one_l, 0, wgc[y, :, :, left]),
            (wg_one_r, 1, wgc[:, x, :, right]),
        ):
            for copy in copies:
                copy.wait_recv()
            value = own.astype(F32)
            for o in (1, 2, 3):
                value += buf1[side, o].astype(F32)
            half2[side] = value.astype(BF16)
        wg_two = [send(half2.at[0, ring(x, o)], buf2.at[0, o], x_dev(o)) for o in (2, 1, 3)]
        wg_two += [send(half2.at[1, ring(y, o)], buf2.at[1, o], y_dev(o)) for o in (2, 1, 3)]

        g_core.wait_recv()
        gacc[...] += grecv[0].astype(F32)
        for g in range(GROUPS):
            cols = slice(g * DH, (g + 1) * DH)
            key_side = gacc[g].astype(BF16)
            dk_ref[:, cols] = (dka[:, cols] + dot(v_ref[:, cols], key_side)).astype(BF16)
            dv_ref[:, cols] = (dva[:, cols] + dot_nt(k_ref[:, cols], key_side)).astype(BF16)

        for copy in z_near:
            copy.wait_recv()
        acc[0:TILE] = piece[z, 0:TILE].astype(F32) + zbuf[4].astype(F32)
        acc[TILE:] = piece[z, TILE:].astype(F32) + zbuf[1].astype(F32)
        for copy in wg_two:
            copy.wait_recv()
        for side, own, span in ((0, x, left), (1, y, right)):
            value = half2[side, own].astype(F32)
            for o in (1, 2, 3):
                value += buf2[side, o].astype(F32)
            wg_ref[:, span] = value * norm

        for copy in z_middle:
            copy.wait_recv()
        proj_ref[0:TILE] = (acc[0:TILE] + zbuf[2].astype(F32)).astype(BF16)
        proj_ref[TILE:] = (acc[TILE:] + zbuf[5].astype(F32)).astype(BF16)
        for copy in sent:
            copy.wait_send()

    return kernel


COPIES = 64


def store(*refs):
    sem = refs[-1]
    copies = [
        pltpu.make_async_copy(refs[i], refs[5 + i], sem.at[i]) for i in range(5)
    ]
    for copy in copies:
        copy.start()
    for copy in copies:
        copy.wait()


def local(queries, key_heads, value_heads, class_ids, level_table, out_weight, out_grad):
    tokens = queries.shape[0]
    norm = (tokens * lax.axis_size("ctx")) ** (-0.5)
    levels = LOCAL + CROSS
    vmem = pl.BlockSpec(memory_space=pltpu.VMEM)
    scratch = [
        pltpu.VMEM((TOKENS, WIDTH), BF16),
        pltpu.VMEM((TOKENS, GROUPS * DH), BF16),
        pltpu.VMEM((TOKENS, GROUPS * DH), BF16),
        pltpu.VMEM((1, TOKENS), jnp.int32),
        pltpu.VMEM((levels, HEADS, level_table.shape[0]), F32),
        pltpu.VMEM((RING, TOKENS, WIDTH), BF16),
        pltpu.VMEM((RING, RING, 2, CH, WIDTH), BF16),
        pltpu.VMEM((TOKENS, WIDTH), F32),
        pltpu.VMEM((TOKENS, WIDTH), BF16),
        pltpu.VMEM((TOKENS, WIDTH), BF16),
        pltpu.VMEM((RING, TOKENS, WIDTH), BF16),
        pltpu.VMEM((6, TILE, WIDTH), BF16),
        pltpu.VMEM((RING, RING, 2, CH, WIDTH), BF16),
        pltpu.VMEM((RING, RING, CH, WIDTH), BF16),
        pltpu.VMEM((2, RING, RING, CH, TILE), BF16),
        pltpu.VMEM((2, RING, CH, TILE), BF16),
        pltpu.VMEM((2, RING, CH, TILE), BF16),
        pltpu.VMEM((HEADS, TOKENS, levels), F32),
        pltpu.VMEM((HEADS, TOKENS, CROSS * DH), BF16),
        pltpu.VMEM((HEADS, 3, TILE, TILE), BF16),
        pltpu.VMEM((GROUPS, DH, DH), F32),
        pltpu.VMEM((3, GROUPS, DH, DH), BF16),
        pltpu.VMEM((7, GROUPS, DH, DH), BF16),
        pltpu.VMEM((GROUPS, CROSS * DH, DH), BF16),
        pltpu.VMEM((GROUPS, DH, CROSS * DH), F32),
        pltpu.VMEM((GROUPS, DH, DH), F32),
        pltpu.VMEM((7, GROUPS, DH, DH), BF16),
        pltpu.VMEM((7, GROUPS, DH, DH), BF16),
        pltpu.VMEM((TOKENS, GROUPS * DH), F32),
        pltpu.VMEM((TOKENS, GROUPS * DH), F32),
        pltpu.SemaphoreType.DMA((7,)),
        pltpu.SemaphoreType.DMA((COPIES,)),
        pltpu.SemaphoreType.DMA((COPIES,)),
    ]
    hbm = pl.BlockSpec(memory_space=pl.ANY)
    shapes = (
        ((TOKENS, WIDTH), BF16),
        ((TOKENS, WIDTH), BF16),
        ((TOKENS, GROUPS * DH), BF16),
        ((TOKENS, GROUPS * DH), BF16),
        ((CH, WIDTH), F32),
    )
    results = pl.pallas_call(
        make_kernel(norm),
        out_shape=tuple(pltpu.VMEM(*shape) for shape in shapes),
        in_specs=[hbm] * 7,
        out_specs=(vmem,) * 5,
        scratch_shapes=scratch,
        compiler_params=pltpu.CompilerParams(
            collective_id=0, has_side_effects=True, vmem_limit_bytes=56 << 20
        ),
        name="layer",
    )(
        queries,
        key_heads,
        value_heads,
        class_ids.reshape(1, tokens),
        level_table.transpose(2, 1, 0),
        out_weight,
        out_grad,
    )
    return pl.pallas_call(
        store,
        out_shape=tuple(jax.ShapeDtypeStruct(*shape) for shape in shapes),
        in_specs=[vmem] * 5,
        out_specs=(pl.BlockSpec(memory_space=pl.ANY),) * 5,
        scratch_shapes=[pltpu.SemaphoreType.DMA((5,))],
        name="store",
    )(*(pltpu.with_memory_space_constraint(result, pltpu.VMEM) for result in results))


def solution(mesh):
    placed = (
        P("ctx", "heads"),
        P("ctx", "heads"),
        P("ctx", "heads"),
        P("ctx"),
        P(None, "heads", None),
        P("ctx", "heads"),
        P("ctx", "heads"),
    )
    return jax.shard_map(
        local,
        mesh=mesh,
        in_specs=placed,
        out_specs=(P("ctx", "heads"),) * 5,
        check_vma=False,
    )
```

```python
import jax
import jax.numpy as jnp
from jax import lax
from jax.experimental import pallas as pl
from jax.experimental.pallas import tpu as pltpu
from jax.sharding import PartitionSpec as P

DH = 128
CH = 64
RING = 4
LOCAL = 4
CROSS = 5
TILE = 256
TOKENS = 512
WIDTH = 512
HEADS = 4
GROUPS = 2
BF16 = jnp.bfloat16
F32 = jnp.float32


def coefficient(level):
    return DH ** (-0.5) * (CH * 2 ** max(level - 1, 0)) ** (-0.5)


def contract(a, b, da, db, precision=None):
    return lax.dot_general(
        a, b, (((da,), (db,)), ((), ())), preferred_element_type=F32, precision=precision
    )


def dot(a, b):
    return contract(a, b, 1, 0)


def dot_nt(a, b):
    return contract(a, b, 1, 1)


def dot_tn(a, b):
    return contract(a, b, 0, 0)


def ring(index, offset):
    return lax.rem(index + offset + RING, RING)


def flag(condition):
    return condition.astype(jnp.int32).astype(F32)


def make_kernel(norm):
    def kernel(
        q_hbm, k_hbm, v_hbm, ids_ref, tab_ref, w_hbm, og_hbm,
        proj_ref, dq_ref, dk_ref, dv_ref, wg_ref,
        q_ref, k_ref, v_ref, ogf, wf, acc, attn, ga, piece, zbuf, wg, wgc, buf1, half2, buf2,
        scale, wqc, prob, total, ssend, srecv, read, gmat, gacc, gsend, grecv, dka, dva,
        lsem, ssem, rsem,
    ):
        z = lax.axis_index("heads")
        c = lax.axis_index("ctx")
        core = lax.rem(c, 2)
        x = lax.rem(c // 2, RING)
        y = c // 8
        used = [0]
        sent = []

        def z_dev(offset):
            return {"heads": ring(z, offset)}

        def x_dev(offset):
            return {"ctx": (y * RING + ring(x, offset)) * 2 + core}

        def y_dev(offset):
            return {"ctx": (ring(y, offset) * RING + x) * 2 + core}

        sibling = {"ctx": (y * RING + x) * 2 + 1 - core}

        def send(src, dst, device):
            number = used[0]
            used[0] = number + 1
            copy = pltpu.make_async_remote_copy(
                src_ref=src,
                dst_ref=dst,
                send_sem=ssem.at[number],
                recv_sem=rsem.at[number],
                device_id=device,
                device_id_type=pl.DeviceIdType.MESH,
            )
            copy.start()
            sent.append(copy)
            return copy

        def gather_start(dev, index, half):
            a = send(half(index, 0), half(index, 0), dev(1))
            return [a, send(half(index, 1), half(index, 1), dev(-1))]

        def gather_rest(dev, index, half):
            d = send(half(index, 1), half(index, 1), dev(1))
            return [d, send(half(index, 0), half(index, 0), dev(-1))]

        def gather_forward(dev, index, half, copies):
            before, after = ring(index, -1), ring(index, 1)
            copies[0].wait_recv()
            a = send(half(before, 0), half(before, 0), dev(1))
            copies[1].wait_recv()
            b = send(half(after, 1), half(after, 1), dev(-1))
            return a, b

        def scatter_far(dev, index, half, buf):
            far = ring(index, 2)
            return (
                send(half(far, 0), buf.at[0], dev(1)),
                send(half(far, 1), buf.at[3], dev(-1)),
            )

        def scatter_near(dev, index, half, buf):
            return (
                send(half(ring(index, 1), 1), buf.at[1], dev(1)),
                send(half(ring(index, -1), 0), buf.at[4], dev(-1)),
            )

        def scatter_middle(dev, index, half, buf, far):
            after, before = half(ring(index, 1), 0), half(ring(index, -1), 1)
            far[0].wait_recv()
            after[...] = (after[...].astype(F32) + buf[0].astype(F32)).astype(BF16)
            a = send(after, buf.at[2], dev(1))
            far[1].wait_recv()
            before[...] = (before[...].astype(F32) + buf[3].astype(F32)).astype(BF16)
            b = send(before, buf.at[5], dev(-1))
            return a, b

        def scatter_wait(near, middle):
            for copy in near + middle:
                copy.wait_recv()

        def scatter_sum(index, half, buf, part):
            own = half(index, part)[...].astype(F32)
            if part == 0:
                return own + buf[2].astype(F32) + buf[4].astype(F32)
            return own + buf[1].astype(F32) + buf[5].astype(F32)

        barrier = pltpu.get_barrier_semaphore()
        peers = [z_dev(1), z_dev(-1), sibling]
        for offset in (1, 2, 3):
            peers += [x_dev(offset), y_dev(offset)]
        for device in peers:
            pl.semaphore_signal(
                barrier, inc=1, device_id=device, device_id_type=pl.DeviceIdType.MESH
            )

        fetched = [
            pltpu.make_async_copy(source, target, lsem.at[i])
            for i, (source, target) in enumerate(
                (
                    (og_hbm, ogf.at[z]),
                    (w_hbm, wf.at[y, x, core]),
                    (k_hbm, k_ref),
                    (v_hbm, v_ref),
                    (q_hbm, q_ref),
                )
            )
        ]
        for copy in fetched:
            copy.start()
        for copy in fetched:
            copy.wait()
        pl.semaphore_wait(barrier, len(peers))

        def og_half(block, part):
            return ogf.at[block, pl.ds(part * TILE, TILE)]

        og_copies = gather_start(z_dev, z, og_half)

        left, right = pl.ds(0, TILE), pl.ds(TILE, TILE)
        mine_l = wf.at[y, x, core, :, left]
        mine_r = wf.at[y, x, core, :, right]
        w_one = [send(mine_l, mine_l, x_dev(o)) for o in (1, 3, 2)]
        w_one += [send(mine_r, mine_r, y_dev(o)) for o in (1, 3, 2)]

        for g in range(GROUPS):
            cols = slice(g * DH, (g + 1) * DH)
            total[g] = dot_tn(k_ref[:, cols], v_ref[:, cols])
        ssend[0] = total[...].astype(BF16)
        s_core = send(ssend.at[0], srecv.at[0], sibling)

        classes = tab_ref.shape[2]
        onehot = (
            lax.broadcasted_iota(jnp.int32, (classes, TOKENS), 0) == ids_ref[...]
        ).astype(F32)
        levels = LOCAL + CROSS
        level = lax.broadcasted_iota(jnp.int32, (1, levels), 1)
        coef = jnp.full((1, levels), coefficient(0), F32)
        for number in range(1, levels):
            coef = jnp.where(level == number, coefficient(number), coef)
        for h in range(HEADS):
            lam = contract(onehot, tab_ref[:, h, :], 0, 1, lax.Precision.HIGHEST)
            scale[h] = lam * coef

        s_core.wait_recv()
        got = srecv[0].astype(F32)
        for g in range(GROUPS):
            read[g, 0:DH] = (got[g] * flag(core == 1)).astype(BF16)
        total[...] += got
        ssend[1] = total[...].astype(BF16)
        s_x = [send(ssend.at[1], srecv.at[o], x_dev(o)) for o in (1, 2, 3)]

        for copy in w_one:
            copy.wait_recv()
        row_l = wf.at[y, :, core, :, left]
        row_r = wf.at[:, x, core, :, right]
        w_two_l = [send(row_l, row_l, y_dev(o)) for o in (1, 3, 2)]
        w_two_r = [send(row_r, row_r, x_dev(o)) for o in (1, 3, 2)]

        og_copies += gather_rest(z_dev, z, og_half)

        def weigh(h):
            cols = pl.ds(pl.multiple_of(h * DH, DH), DH)
            q = q_ref[:, cols].astype(F32)
            for l in range(CROSS):
                wqc[h, :, l * DH : (l + 1) * DH] = (
                    q * scale[h, :, LOCAL + l : LOCAL + l + 1]
                ).astype(BF16)

        lax.fori_loop(0, HEADS, lambda h, _: (weigh(h), 0)[1], 0)

        og_far = gather_forward(z_dev, z, og_half, og_copies)

        def exchange(copies, position, slot, low):
            near = jnp.zeros((GROUPS, DH, DH), F32)
            far = jnp.zeros((GROUPS, DH, DH), F32)
            everything = total[...]
            for o, copy in zip((1, 2, 3), copies):
                copy.wait_recv()
                source = ring(position, -o)
                value = srecv[slot + o].astype(F32)
                upper = source < position
                same = source // 2 == position // 2
                near += value * flag(jnp.logical_and(upper, same))
                far += value * flag(jnp.logical_and(upper, jnp.logical_not(same)))
                everything += value
            for g in range(GROUPS):
                read[g, low * DH : (low + 1) * DH] = near[g].astype(BF16)
                read[g, (low + 1) * DH : (low + 2) * DH] = far[g].astype(BF16)
            total[...] = everything

        exchange(s_x, x, 0, 1)
        ssend[2] = total[...].astype(BF16)
        s_y = [send(ssend.at[2], srecv.at[3 + o], y_dev(o)) for o in (1, 2, 3)]

        rows = lax.broadcasted_iota(jnp.int32, (TILE, TILE), 0)
        cols_ = lax.broadcasted_iota(jnp.int32, (TILE, TILE), 1)

        def tile_weight(h, i):
            span = pl.ds(i * TILE, TILE)
            weight = jnp.where(
                rows // (2 * CH) > cols_ // (2 * CH), scale[h, span, 2:3], 0.0
            )
            weight = jnp.where(
                jnp.logical_and(
                    rows // (2 * CH) == cols_ // (2 * CH), rows // CH > cols_ // CH
                ),
                scale[h, span, 1:2],
                weight,
            )
            return jnp.where(
                jnp.logical_and(rows // CH == cols_ // CH, rows >= cols_),
                scale[h, span, 0:1],
                weight,
            )

        first, second = pl.ds(0, TILE), pl.ds(TILE, TILE)

        def forward(h):
            cols = pl.ds(pl.multiple_of(h * DH, DH), DH)
            group = pl.ds(pl.multiple_of(h // 2 * DH, DH), DH)
            q0, q1 = q_ref[first, cols], q_ref[second, cols]
            k0, k1 = k_ref[first, group], k_ref[second, group]
            v0, v1 = v_ref[first, group], v_ref[second, group]
            p0 = (dot_nt(q0, k0) * tile_weight(h, 0)).astype(BF16)
            p1 = (dot_nt(q1, k1) * tile_weight(h, 1)).astype(BF16)
            p2 = (dot_nt(q1, k0) * scale[h, second, 3:4]).astype(BF16)
            prob[h, 0] = p0
            prob[h, 1] = p1
            prob[h, 2] = p2
            acc[first, cols] = dot(p0, v0)
            acc[second, cols] = dot(p1, v1) + dot(p2, v0)

        lax.fori_loop(0, HEADS, lambda h, _: (forward(h), 0)[1], 0)
        w_core = []
        for copies, span in ((w_two_l, left), (w_two_r, right)):
            for copy in copies:
                copy.wait_recv()
            part = wf.at[:, :, core, :, span]
            w_core.append(send(part, part, sibling))
        exchange(s_y, y, 3, 3)

        def across(h):
            cols = pl.ds(pl.multiple_of(h * DH, DH), DH)
            attn[:, cols] = (acc[:, cols] + dot(wqc[h], read[h // 2])).astype(BF16)

        lax.fori_loop(0, HEADS, lambda h, _: (across(h), 0)[1], 0)

        wg_core = []

        def weight_grad(block):
            term = dot_tn(ogf[block], attn[...]).astype(BF16)
            wg[block] = term.reshape(RING, 2, CH, WIDTH)
            wg_core.append(send(wg.at[block, :, 1 - core], wgc.at[block], sibling))

        weight_grad(z)
        og_copies[2].wait_recv()
        weight_grad(ring(z, -1))
        og_copies[3].wait_recv()
        weight_grad(ring(z, 1))
        for copy in w_core:
            copy.wait_recv()

        def weights(block):
            return wf[block].reshape(WIDTH, WIDTH)

        def project(block):
            piece[block] = dot_nt(attn[...], weights(block)).astype(BF16)

        def z_half(block, part):
            return piece.at[block, pl.ds(part * TILE, TILE)]

        def back(block):
            return dot(ogf[block], weights(block))

        wg_one_r = []

        def merge(number, block):
            wg_core[number].wait_recv()
            wgc[block] = (wg[block, :, core].astype(F32) + wgc[block].astype(F32)).astype(BF16)
            for o in (2, 1, 3):
                wg_one_r.append(
                    send(wgc.at[block, ring(x, o), :, right], buf1.at[1, o, block], x_dev(o))
                )

        project(ring(z, 2))
        z_far = scatter_far(z_dev, z, z_half, zbuf)
        acc[...] = back(z) + back(ring(z, -1)) + back(ring(z, 1))
        merge(0, z)
        merge(1, ring(z, -1))
        merge(2, ring(z, 1))
        og_far[0].wait_recv()
        og_far[1].wait_recv()
        ga[...] = (acc[...] + back(ring(z, 2))).astype(BF16)
        weight_grad(ring(z, 2))

        def state_grad(g):
            value = jnp.zeros((DH, CROSS * DH), F32)
            for r in range(2):
                h = g * 2 + r
                cols = pl.ds(pl.multiple_of(h * DH, DH), DH)
                value += dot_tn(ga[:, cols], wqc[h])
            gmat[g] = value

        lax.fori_loop(0, GROUPS, lambda g, _: (state_grad(g), 0)[1], 0)

        def level_grad(number):
            return gmat[:, :, number * DH : (number + 1) * DH]

        g_y = []
        for o in (1, 2, 3):
            same = flag(y // 2 == ring(y, o) // 2)
            gsend[o] = (level_grad(3) * same + level_grad(4) * (1.0 - same)).astype(BF16)
            g_y.append(send(gsend.at[o], grecv.at[o], y_dev(o)))

        project(ring(z, 1))
        project(ring(z, -1))
        z_near = scatter_near(z_dev, z, z_half, zbuf)

        merge(3, ring(z, 2))
        wg_one_l = [
            send(wgc.at[ring(y, o), :, :, left], buf1.at[0, o], y_dev(o)) for o in (2, 1, 3)
        ]
        project(z)
        gacc[...] = jnp.zeros_like(gacc)
        for o, copy in zip((1, 2, 3), g_y):
            copy.wait_recv()
            gacc[...] += grecv[o].astype(F32) * flag(ring(y, -o) > y)
        g_x = []
        for o in (1, 2, 3):
            same = flag(x // 2 == ring(x, o) // 2)
            lower = flag(x > ring(x, o))
            gsend[3 + o] = (
                gacc[...]
                + level_grad(1) * (lower * same)
                + level_grad(2) * (lower * (1.0 - same))
            ).astype(BF16)
            g_x.append(send(gsend.at[3 + o], grecv.at[3 + o], x_dev(o)))

        def backward(g):
            group = pl.ds(pl.multiple_of(g * DH, DH), DH)
            k0, k1 = k_ref[first, group], k_ref[second, group]
            v0, v1 = v_ref[first, group], v_ref[second, group]
            for r in range(2):
                h = g * 2 + r
                cols = pl.ds(pl.multiple_of(h * DH, DH), DH)
                q0, q1 = q_ref[first, cols], q_ref[second, cols]
                g0, g1 = ga[first, cols], ga[second, cols]
                d0 = (dot_nt(g0, v0) * tile_weight(h, 0)).astype(BF16)
                d1 = (dot_nt(g1, v1) * tile_weight(h, 1)).astype(BF16)
                d2 = (dot_nt(g1, v0) * scale[h, second, 3:4]).astype(BF16)
                dq0 = dot(d0, k0)
                dq1 = dot(d1, k1) + dot(d2, k0)
                y0, y1 = dot_nt(g0, read[g]), dot_nt(g1, read[g])
                for l in range(CROSS):
                    part = slice(l * DH, (l + 1) * DH)
                    number = slice(LOCAL + l, LOCAL + l + 1)
                    dq0 += y0[:, part] * scale[h, first, number]
                    dq1 += y1[:, part] * scale[h, second, number]
                dq_ref[first, cols] = dq0.astype(BF16)
                dq_ref[second, cols] = dq1.astype(BF16)
                p0, p1, p2 = prob[h, 0], prob[h, 1], prob[h, 2]
                dk0 = dot_tn(d0, q0) + dot_tn(d2, q1)
                dk1 = dot_tn(d1, q1)
                dv0 = dot_tn(p0, g0) + dot_tn(p2, g1)
                dv1 = dot_tn(p1, g1)
                if r == 0:
                    dka[first, group] = dk0
                    dka[second, group] = dk1
                    dva[first, group] = dv0
                    dva[second, group] = dv1
                else:
                    dka[first, group] += dk0
                    dka[second, group] += dk1
                    dva[first, group] += dv0
                    dva[second, group] += dv1

        backward_loop = lambda a, b: lax.fori_loop(a, b, lambda g, _: (backward(g), 0)[1], 0)
        backward_loop(0, 1)
        z_middle = scatter_middle(z_dev, z, z_half, zbuf, z_far)
        backward_loop(1, 2)
        for o, copy in zip((1, 2, 3), g_x):
            copy.wait_recv()
            gacc[...] += grecv[3 + o].astype(F32)
        gsend[0] = (gacc[...] + level_grad(0) * flag(core == 1)).astype(BF16)
        g_core = send(gsend.at[0], grecv.at[0], sibling)

        for copies, side, own in (
            (wg_one_l, 0, wgc[y, :, :, left]),
            (wg_one_r, 1, wgc[:, x, :, right]),
        ):
            for copy in copies:
                copy.wait_recv()
            value = own.astype(F32)
            for o in (1, 2, 3):
                value += buf1[side, o].astype(F32)
            half2[side] = value.astype(BF16)
        wg_two = [send(half2.at[0, ring(x, o)], buf2.at[0, o], x_dev(o)) for o in (2, 1, 3)]
        wg_two += [send(half2.at[1, ring(y, o)], buf2.at[1, o], y_dev(o)) for o in (2, 1, 3)]

        g_core.wait_recv()
        gacc[...] += grecv[0].astype(F32)
        for g in range(GROUPS):
            cols = slice(g * DH, (g + 1) * DH)
            key_side = gacc[g].astype(BF16)
            dk_ref[:, cols] = (dka[:, cols] + dot(v_ref[:, cols], key_side)).astype(BF16)
            dv_ref[:, cols] = (dva[:, cols] + dot_nt(k_ref[:, cols], key_side)).astype(BF16)

        for copy in wg_two:
            copy.wait_recv()
        for side, own, span in ((0, x, left), (1, y, right)):
            value = half2[side, own].astype(F32)
            for o in (1, 2, 3):
                value += buf2[side, o].astype(F32)
            wg_ref[:, span] = value * norm

        scatter_wait(z_near, z_middle)
        proj_ref[0:TILE] = scatter_sum(z, z_half, zbuf, 0).astype(BF16)
        proj_ref[TILE:] = scatter_sum(z, z_half, zbuf, 1).astype(BF16)
        for copy in sent:
            copy.wait_send()

    return kernel


COPIES = 72


def store(*refs):
    sem = refs[-1]
    copies = [
        pltpu.make_async_copy(refs[i], refs[5 + i], sem.at[i]) for i in range(5)
    ]
    for copy in copies:
        copy.start()
    for copy in copies:
        copy.wait()


def local(queries, key_heads, value_heads, class_ids, level_table, out_weight, out_grad):
    tokens = queries.shape[0]
    norm = (tokens * lax.axis_size("ctx")) ** (-0.5)
    levels = LOCAL + CROSS
    vmem = pl.BlockSpec(memory_space=pltpu.VMEM)
    scratch = [
        pltpu.VMEM((TOKENS, WIDTH), BF16),
        pltpu.VMEM((TOKENS, GROUPS * DH), BF16),
        pltpu.VMEM((TOKENS, GROUPS * DH), BF16),
        pltpu.VMEM((RING, TOKENS, WIDTH), BF16),
        pltpu.VMEM((RING, RING, 2, CH, WIDTH), BF16),
        pltpu.VMEM((TOKENS, WIDTH), F32),
        pltpu.VMEM((TOKENS, WIDTH), BF16),
        pltpu.VMEM((TOKENS, WIDTH), BF16),
        pltpu.VMEM((RING, TOKENS, WIDTH), BF16),
        pltpu.VMEM((6, TILE, WIDTH), BF16),
        pltpu.VMEM((RING, RING, 2, CH, WIDTH), BF16),
        pltpu.VMEM((RING, RING, CH, WIDTH), BF16),
        pltpu.VMEM((2, RING, RING, CH, TILE), BF16),
        pltpu.VMEM((2, RING, CH, TILE), BF16),
        pltpu.VMEM((2, RING, CH, TILE), BF16),
        pltpu.VMEM((HEADS, TOKENS, levels), F32),
        pltpu.VMEM((HEADS, TOKENS, CROSS * DH), BF16),
        pltpu.VMEM((HEADS, 3, TILE, TILE), BF16),
        pltpu.VMEM((GROUPS, DH, DH), F32),
        pltpu.VMEM((3, GROUPS, DH, DH), BF16),
        pltpu.VMEM((7, GROUPS, DH, DH), BF16),
        pltpu.VMEM((GROUPS, CROSS * DH, DH), BF16),
        pltpu.VMEM((GROUPS, DH, CROSS * DH), F32),
        pltpu.VMEM((GROUPS, DH, DH), F32),
        pltpu.VMEM((7, GROUPS, DH, DH), BF16),
        pltpu.VMEM((7, GROUPS, DH, DH), BF16),
        pltpu.VMEM((TOKENS, GROUPS * DH), F32),
        pltpu.VMEM((TOKENS, GROUPS * DH), F32),
        pltpu.SemaphoreType.DMA((5,)),
        pltpu.SemaphoreType.DMA((COPIES,)),
        pltpu.SemaphoreType.DMA((COPIES,)),
    ]
    hbm = pl.BlockSpec(memory_space=pl.ANY)
    shapes = (
        ((TOKENS, WIDTH), BF16),
        ((TOKENS, WIDTH), BF16),
        ((TOKENS, GROUPS * DH), BF16),
        ((TOKENS, GROUPS * DH), BF16),
        ((CH, WIDTH), F32),
    )
    results = pl.pallas_call(
        make_kernel(norm),
        out_shape=tuple(pltpu.VMEM(*shape) for shape in shapes),
        in_specs=[hbm, hbm, hbm, vmem, vmem, hbm, hbm],
        out_specs=(vmem,) * 5,
        scratch_shapes=scratch,
        compiler_params=pltpu.CompilerParams(
            collective_id=0, has_side_effects=True, vmem_limit_bytes=56 << 20
        ),
        name="layer",
    )(
        queries,
        key_heads,
        value_heads,
        class_ids.reshape(1, tokens),
        level_table.transpose(2, 1, 0),
        out_weight,
        out_grad,
    )
    return pl.pallas_call(
        store,
        out_shape=tuple(jax.ShapeDtypeStruct(*shape) for shape in shapes),
        in_specs=[vmem] * 5,
        out_specs=(pl.BlockSpec(memory_space=pl.ANY),) * 5,
        scratch_shapes=[pltpu.SemaphoreType.DMA((5,))],
        name="store",
    )(*(pltpu.with_memory_space_constraint(result, pltpu.VMEM) for result in results))


def solution(mesh):
    placed = (
        P("ctx", "heads"),
        P("ctx", "heads"),
        P("ctx", "heads"),
        P("ctx"),
        P(None, "heads", None),
        P("ctx", "heads"),
        P("ctx", "heads"),
    )
    return jax.shard_map(
        local,
        mesh=mesh,
        in_specs=placed,
        out_specs=(P("ctx", "heads"),) * 5,
        check_vma=False,
    )
```

```python
import jax
import jax.numpy as jnp
from jax import lax
from jax.experimental import pallas as pl
from jax.experimental.pallas import tpu as pltpu
from jax.sharding import PartitionSpec as P

DH = 128
CH = 64
RING = 4
LOCAL = 4
CROSS = 5
TILE = 256
TOKENS = 512
WIDTH = 512
HEADS = 4
GROUPS = 2
BF16 = jnp.bfloat16
F32 = jnp.float32


def coefficient(level):
    return DH ** (-0.5) * (CH * 2 ** max(level - 1, 0)) ** (-0.5)


def contract(a, b, da, db, precision=None):
    return lax.dot_general(
        a, b, (((da,), (db,)), ((), ())), preferred_element_type=F32, precision=precision
    )


def dot(a, b):
    return contract(a, b, 1, 0)


def dot_nt(a, b):
    return contract(a, b, 1, 1)


def dot_tn(a, b):
    return contract(a, b, 0, 0)


def ring(index, offset):
    return lax.rem(index + offset + RING, RING)


def flag(condition):
    return condition.astype(jnp.int32).astype(F32)


def make_kernel(norm):
    def kernel(
        q_hbm, k_hbm, v_hbm, ids_hbm, tab_hbm, w_hbm, og_hbm,
        proj_ref, dq_ref, dk_ref, dv_ref, wg_ref,
        q_ref, k_ref, v_ref, ids_ref, tab_ref, ogf, wf, acc, attn, ga, piece, zbuf, wg, wgc, buf1, half2, buf2,
        scale, wqc, prob, total, ssend, srecv, read, gmat, gacc, gsend, grecv, dka, dva,
        lsem, ssem, rsem,
    ):
        z = lax.axis_index("heads")
        c = lax.axis_index("ctx")
        core = lax.rem(c, 2)
        x = lax.rem(c // 2, RING)
        y = c // 8
        used = [0]
        sent = []

        def z_dev(offset):
            return {"heads": ring(z, offset)}

        def x_dev(offset):
            return {"ctx": (y * RING + ring(x, offset)) * 2 + core}

        def y_dev(offset):
            return {"ctx": (ring(y, offset) * RING + x) * 2 + core}

        sibling = {"ctx": (y * RING + x) * 2 + 1 - core}

        def send(src, dst, device):
            number = used[0]
            used[0] = number + 1
            copy = pltpu.make_async_remote_copy(
                src_ref=src,
                dst_ref=dst,
                send_sem=ssem.at[number],
                recv_sem=rsem.at[number],
                device_id=device,
                device_id_type=pl.DeviceIdType.MESH,
            )
            copy.start()
            sent.append(copy)
            return copy

        def gather_start(dev, index, half):
            a = send(half(index, 0), half(index, 0), dev(1))
            return [a, send(half(index, 1), half(index, 1), dev(-1))]

        def gather_rest(dev, index, half):
            d = send(half(index, 1), half(index, 1), dev(1))
            return [d, send(half(index, 0), half(index, 0), dev(-1))]

        def gather_forward(dev, index, half, copies):
            before, after = ring(index, -1), ring(index, 1)
            copies[0].wait_recv()
            a = send(half(before, 0), half(before, 0), dev(1))
            copies[1].wait_recv()
            b = send(half(after, 1), half(after, 1), dev(-1))
            return a, b

        def scatter_far(dev, index, half, buf):
            far = ring(index, 2)
            return (
                send(half(far, 0), buf.at[0], dev(1)),
                send(half(far, 1), buf.at[3], dev(-1)),
            )

        def scatter_near(dev, index, half, buf):
            return (
                send(half(ring(index, 1), 1), buf.at[1], dev(1)),
                send(half(ring(index, -1), 0), buf.at[4], dev(-1)),
            )

        def scatter_middle(dev, index, half, buf, far):
            after, before = half(ring(index, 1), 0), half(ring(index, -1), 1)
            far[0].wait_recv()
            after[...] = (after[...].astype(F32) + buf[0].astype(F32)).astype(BF16)
            a = send(after, buf.at[2], dev(1))
            far[1].wait_recv()
            before[...] = (before[...].astype(F32) + buf[3].astype(F32)).astype(BF16)
            b = send(before, buf.at[5], dev(-1))
            return a, b

        def scatter_wait(near, middle):
            for copy in near + middle:
                copy.wait_recv()

        def scatter_sum(index, half, buf, part):
            own = half(index, part)[...].astype(F32)
            if part == 0:
                return own + buf[2].astype(F32) + buf[4].astype(F32)
            return own + buf[1].astype(F32) + buf[5].astype(F32)

        barrier = pltpu.get_barrier_semaphore()
        peers = [z_dev(1), z_dev(-1), sibling]
        for offset in (1, 2, 3):
            peers += [x_dev(offset), y_dev(offset)]
        for device in peers:
            pl.semaphore_signal(
                barrier, inc=1, device_id=device, device_id_type=pl.DeviceIdType.MESH
            )

        fetched = [
            pltpu.make_async_copy(source, target, lsem.at[i])
            for i, (source, target) in enumerate(
                (
                    (og_hbm, ogf.at[z]),
                    (w_hbm, wf.at[y, x, core]),
                    (k_hbm, k_ref),
                    (v_hbm, v_ref),
                    (q_hbm, q_ref),
                    (ids_hbm, ids_ref),
                    (tab_hbm, tab_ref),
                )
            )
        ]
        for copy in fetched:
            copy.start()
        fetched[0].wait()
        fetched[1].wait()
        pl.semaphore_wait(barrier, len(peers))

        def og_half(block, part):
            return ogf.at[block, pl.ds(part * TILE, TILE)]

        og_copies = gather_start(z_dev, z, og_half)

        left, right = pl.ds(0, TILE), pl.ds(TILE, TILE)
        mine_l = wf.at[y, x, core, :, left]
        mine_r = wf.at[y, x, core, :, right]
        w_one = [send(mine_l, mine_l, x_dev(o)) for o in (1, 3, 2)]
        w_one += [send(mine_r, mine_r, y_dev(o)) for o in (1, 3, 2)]

        fetched[2].wait()
        fetched[3].wait()
        for g in range(GROUPS):
            cols = slice(g * DH, (g + 1) * DH)
            total[g] = dot_tn(k_ref[:, cols], v_ref[:, cols])
        ssend[0] = total[...].astype(BF16)
        s_core = send(ssend.at[0], srecv.at[0], sibling)

        for copy in fetched[4:]:
            copy.wait()
        classes = tab_ref.shape[2]
        onehot = (
            lax.broadcasted_iota(jnp.int32, (classes, TOKENS), 0) == ids_ref[...]
        ).astype(F32)
        levels = LOCAL + CROSS
        level = lax.broadcasted_iota(jnp.int32, (1, levels), 1)
        coef = jnp.full((1, levels), coefficient(0), F32)
        for number in range(1, levels):
            coef = jnp.where(level == number, coefficient(number), coef)
        for h in range(HEADS):
            lam = contract(onehot, tab_ref[:, h, :], 0, 1, lax.Precision.HIGHEST)
            scale[h] = lam * coef

        s_core.wait_recv()
        got = srecv[0].astype(F32)
        for g in range(GROUPS):
            read[g, 0:DH] = (got[g] * flag(core == 1)).astype(BF16)
        total[...] += got
        ssend[1] = total[...].astype(BF16)
        s_x = [send(ssend.at[1], srecv.at[o], x_dev(o)) for o in (1, 2, 3)]

        for copy in w_one:
            copy.wait_recv()
        row_l = wf.at[y, :, core, :, left]
        row_r = wf.at[:, x, core, :, right]
        w_two_l = [send(row_l, row_l, y_dev(o)) for o in (1, 3, 2)]
        w_two_r = [send(row_r, row_r, x_dev(o)) for o in (1, 3, 2)]

        og_copies += gather_rest(z_dev, z, og_half)

        def weigh(h):
            cols = pl.ds(pl.multiple_of(h * DH, DH), DH)
            q = q_ref[:, cols].astype(F32)
            for l in range(CROSS):
                wqc[h, :, l * DH : (l + 1) * DH] = (
                    q * scale[h, :, LOCAL + l : LOCAL + l + 1]
                ).astype(BF16)

        lax.fori_loop(0, HEADS, lambda h, _: (weigh(h), 0)[1], 0)

        og_far = gather_forward(z_dev, z, og_half, og_copies)

        def exchange(copies, position, slot, low):
            near = jnp.zeros((GROUPS, DH, DH), F32)
            far = jnp.zeros((GROUPS, DH, DH), F32)
            everything = total[...]
            for o, copy in zip((1, 2, 3), copies):
                copy.wait_recv()
                source = ring(position, -o)
                value = srecv[slot + o].astype(F32)
                upper = source < position
                same = source // 2 == position // 2
                near += value * flag(jnp.logical_and(upper, same))
                far += value * flag(jnp.logical_and(upper, jnp.logical_not(same)))
                everything += value
            for g in range(GROUPS):
                read[g, low * DH : (low + 1) * DH] = near[g].astype(BF16)
                read[g, (low + 1) * DH : (low + 2) * DH] = far[g].astype(BF16)
            total[...] = everything

        exchange(s_x, x, 0, 1)
        ssend[2] = total[...].astype(BF16)
        s_y = [send(ssend.at[2], srecv.at[3 + o], y_dev(o)) for o in (1, 2, 3)]

        rows = lax.broadcasted_iota(jnp.int32, (TILE, TILE), 0)
        cols_ = lax.broadcasted_iota(jnp.int32, (TILE, TILE), 1)

        def tile_weight(h, i):
            span = pl.ds(i * TILE, TILE)
            weight = jnp.where(
                rows // (2 * CH) > cols_ // (2 * CH), scale[h, span, 2:3], 0.0
            )
            weight = jnp.where(
                jnp.logical_and(
                    rows // (2 * CH) == cols_ // (2 * CH), rows // CH > cols_ // CH
                ),
                scale[h, span, 1:2],
                weight,
            )
            return jnp.where(
                jnp.logical_and(rows // CH == cols_ // CH, rows >= cols_),
                scale[h, span, 0:1],
                weight,
            )

        first, second = pl.ds(0, TILE), pl.ds(TILE, TILE)

        def forward(h):
            cols = pl.ds(pl.multiple_of(h * DH, DH), DH)
            group = pl.ds(pl.multiple_of(h // 2 * DH, DH), DH)
            q0, q1 = q_ref[first, cols], q_ref[second, cols]
            k0, k1 = k_ref[first, group], k_ref[second, group]
            v0, v1 = v_ref[first, group], v_ref[second, group]
            p0 = (dot_nt(q0, k0) * tile_weight(h, 0)).astype(BF16)
            p1 = (dot_nt(q1, k1) * tile_weight(h, 1)).astype(BF16)
            p2 = (dot_nt(q1, k0) * scale[h, second, 3:4]).astype(BF16)
            prob[h, 0] = p0
            prob[h, 1] = p1
            prob[h, 2] = p2
            acc[first, cols] = dot(p0, v0)
            acc[second, cols] = dot(p1, v1) + dot(p2, v0)

        lax.fori_loop(0, HEADS, lambda h, _: (forward(h), 0)[1], 0)
        w_core = []
        for copies, span in ((w_two_l, left), (w_two_r, right)):
            for copy in copies:
                copy.wait_recv()
            part = wf.at[:, :, core, :, span]
            w_core.append(send(part, part, sibling))
        exchange(s_y, y, 3, 3)

        def across(h):
            cols = pl.ds(pl.multiple_of(h * DH, DH), DH)
            attn[:, cols] = (acc[:, cols] + dot(wqc[h], read[h // 2])).astype(BF16)

        lax.fori_loop(0, HEADS, lambda h, _: (across(h), 0)[1], 0)

        wg_core = []

        def weight_grad(block):
            term = dot_tn(ogf[block], attn[...]).astype(BF16)
            wg[block] = term.reshape(RING, 2, CH, WIDTH)
            wg_core.append(send(wg.at[block, :, 1 - core], wgc.at[block], sibling))

        weight_grad(z)
        og_copies[2].wait_recv()
        weight_grad(ring(z, -1))
        og_copies[3].wait_recv()
        weight_grad(ring(z, 1))
        for copy in w_core:
            copy.wait_recv()

        def weights(block):
            return wf[block].reshape(WIDTH, WIDTH)

        def project(block):
            piece[block] = dot_nt(attn[...], weights(block)).astype(BF16)

        def z_half(block, part):
            return piece.at[block, pl.ds(part * TILE, TILE)]

        def back(block):
            return dot(ogf[block], weights(block))

        wg_one_r = []

        def merge(number, block):
            wg_core[number].wait_recv()
            wgc[block] = (wg[block, :, core].astype(F32) + wgc[block].astype(F32)).astype(BF16)
            for o in (2, 1, 3):
                wg_one_r.append(
                    send(wgc.at[block, ring(x, o), :, right], buf1.at[1, o, block], x_dev(o))
                )

        project(ring(z, 2))
        z_far = scatter_far(z_dev, z, z_half, zbuf)
        acc[...] = back(z) + back(ring(z, -1)) + back(ring(z, 1))
        merge(0, z)
        merge(1, ring(z, -1))
        merge(2, ring(z, 1))
        og_far[0].wait_recv()
        og_far[1].wait_recv()
        ga[...] = (acc[...] + back(ring(z, 2))).astype(BF16)
        weight_grad(ring(z, 2))

        def state_grad(g):
            value = jnp.zeros((DH, CROSS * DH), F32)
            for r in range(2):
                h = g * 2 + r
                cols = pl.ds(pl.multiple_of(h * DH, DH), DH)
                value += dot_tn(ga[:, cols], wqc[h])
            gmat[g] = value

        lax.fori_loop(0, GROUPS, lambda g, _: (state_grad(g), 0)[1], 0)

        def level_grad(number):
            return gmat[:, :, number * DH : (number + 1) * DH]

        g_y = []
        for o in (1, 2, 3):
            same = flag(y // 2 == ring(y, o) // 2)
            gsend[o] = (level_grad(3) * same + level_grad(4) * (1.0 - same)).astype(BF16)
            g_y.append(send(gsend.at[o], grecv.at[o], y_dev(o)))

        project(ring(z, 1))
        project(ring(z, -1))
        z_near = scatter_near(z_dev, z, z_half, zbuf)

        merge(3, ring(z, 2))
        wg_one_l = [
            send(wgc.at[ring(y, o), :, :, left], buf1.at[0, o], y_dev(o)) for o in (2, 1, 3)
        ]
        project(z)
        gacc[...] = jnp.zeros_like(gacc)
        for o, copy in zip((1, 2, 3), g_y):
            copy.wait_recv()
            gacc[...] += grecv[o].astype(F32) * flag(ring(y, -o) > y)
        g_x = []
        for o in (1, 2, 3):
            same = flag(x // 2 == ring(x, o) // 2)
            lower = flag(x > ring(x, o))
            gsend[3 + o] = (
                gacc[...]
                + level_grad(1) * (lower * same)
                + level_grad(2) * (lower * (1.0 - same))
            ).astype(BF16)
            g_x.append(send(gsend.at[3 + o], grecv.at[3 + o], x_dev(o)))

        def backward(g):
            group = pl.ds(pl.multiple_of(g * DH, DH), DH)
            k0, k1 = k_ref[first, group], k_ref[second, group]
            v0, v1 = v_ref[first, group], v_ref[second, group]
            for r in range(2):
                h = g * 2 + r
                cols = pl.ds(pl.multiple_of(h * DH, DH), DH)
                q0, q1 = q_ref[first, cols], q_ref[second, cols]
                g0, g1 = ga[first, cols], ga[second, cols]
                d0 = (dot_nt(g0, v0) * tile_weight(h, 0)).astype(BF16)
                d1 = (dot_nt(g1, v1) * tile_weight(h, 1)).astype(BF16)
                d2 = (dot_nt(g1, v0) * scale[h, second, 3:4]).astype(BF16)
                dq0 = dot(d0, k0)
                dq1 = dot(d1, k1) + dot(d2, k0)
                y0, y1 = dot_nt(g0, read[g]), dot_nt(g1, read[g])
                for l in range(CROSS):
                    part = slice(l * DH, (l + 1) * DH)
                    number = slice(LOCAL + l, LOCAL + l + 1)
                    dq0 += y0[:, part] * scale[h, first, number]
                    dq1 += y1[:, part] * scale[h, second, number]
                dq_ref[first, cols] = dq0.astype(BF16)
                dq_ref[second, cols] = dq1.astype(BF16)
                p0, p1, p2 = prob[h, 0], prob[h, 1], prob[h, 2]
                dk0 = dot_tn(d0, q0) + dot_tn(d2, q1)
                dk1 = dot_tn(d1, q1)
                dv0 = dot_tn(p0, g0) + dot_tn(p2, g1)
                dv1 = dot_tn(p1, g1)
                if r == 0:
                    dka[first, group] = dk0
                    dka[second, group] = dk1
                    dva[first, group] = dv0
                    dva[second, group] = dv1
                else:
                    dka[first, group] += dk0
                    dka[second, group] += dk1
                    dva[first, group] += dv0
                    dva[second, group] += dv1

        backward_loop = lambda a, b: lax.fori_loop(a, b, lambda g, _: (backward(g), 0)[1], 0)
        backward_loop(0, 1)
        z_middle = scatter_middle(z_dev, z, z_half, zbuf, z_far)
        backward_loop(1, 2)
        for o, copy in zip((1, 2, 3), g_x):
            copy.wait_recv()
            gacc[...] += grecv[3 + o].astype(F32)
        gsend[0] = (gacc[...] + level_grad(0) * flag(core == 1)).astype(BF16)
        g_core = send(gsend.at[0], grecv.at[0], sibling)

        for copies, side, own in (
            (wg_one_l, 0, wgc[y, :, :, left]),
            (wg_one_r, 1, wgc[:, x, :, right]),
        ):
            for copy in copies:
                copy.wait_recv()
            value = own.astype(F32)
            for o in (1, 2, 3):
                value += buf1[side, o].astype(F32)
            half2[side] = value.astype(BF16)
        wg_two = [send(half2.at[0, ring(x, o)], buf2.at[0, o], x_dev(o)) for o in (2, 1, 3)]
        wg_two += [send(half2.at[1, ring(y, o)], buf2.at[1, o], y_dev(o)) for o in (2, 1, 3)]

        g_core.wait_recv()
        gacc[...] += grecv[0].astype(F32)
        for g in range(GROUPS):
            cols = slice(g * DH, (g + 1) * DH)
            key_side = gacc[g].astype(BF16)
            dk_ref[:, cols] = (dka[:, cols] + dot(v_ref[:, cols], key_side)).astype(BF16)
            dv_ref[:, cols] = (dva[:, cols] + dot_nt(k_ref[:, cols], key_side)).astype(BF16)

        for copy in wg_two:
            copy.wait_recv()
        for side, own, span in ((0, x, left), (1, y, right)):
            value = half2[side, own].astype(F32)
            for o in (1, 2, 3):
                value += buf2[side, o].astype(F32)
            wg_ref[:, span] = value * norm

        scatter_wait(z_near, z_middle)
        proj_ref[0:TILE] = scatter_sum(z, z_half, zbuf, 0).astype(BF16)
        proj_ref[TILE:] = scatter_sum(z, z_half, zbuf, 1).astype(BF16)
        for copy in sent:
            copy.wait_send()

    return kernel


COPIES = 72


def store(*refs):
    sem = refs[-1]
    copies = [
        pltpu.make_async_copy(refs[i], refs[5 + i], sem.at[i]) for i in range(5)
    ]
    for copy in copies:
        copy.start()
    for copy in copies:
        copy.wait()


def local(queries, key_heads, value_heads, class_ids, level_table, out_weight, out_grad):
    tokens = queries.shape[0]
    norm = (tokens * lax.axis_size("ctx")) ** (-0.5)
    levels = LOCAL + CROSS
    vmem = pl.BlockSpec(memory_space=pltpu.VMEM)
    scratch = [
        pltpu.VMEM((TOKENS, WIDTH), BF16),
        pltpu.VMEM((TOKENS, GROUPS * DH), BF16),
        pltpu.VMEM((TOKENS, GROUPS * DH), BF16),
        pltpu.VMEM((1, TOKENS), jnp.int32),
        pltpu.VMEM((levels, HEADS, level_table.shape[0]), F32),
        pltpu.VMEM((RING, TOKENS, WIDTH), BF16),
        pltpu.VMEM((RING, RING, 2, CH, WIDTH), BF16),
        pltpu.VMEM((TOKENS, WIDTH), F32),
        pltpu.VMEM((TOKENS, WIDTH), BF16),
        pltpu.VMEM((TOKENS, WIDTH), BF16),
        pltpu.VMEM((RING, TOKENS, WIDTH), BF16),
        pltpu.VMEM((6, TILE, WIDTH), BF16),
        pltpu.VMEM((RING, RING, 2, CH, WIDTH), BF16),
        pltpu.VMEM((RING, RING, CH, WIDTH), BF16),
        pltpu.VMEM((2, RING, RING, CH, TILE), BF16),
        pltpu.VMEM((2, RING, CH, TILE), BF16),
        pltpu.VMEM((2, RING, CH, TILE), BF16),
        pltpu.VMEM((HEADS, TOKENS, levels), F32),
        pltpu.VMEM((HEADS, TOKENS, CROSS * DH), BF16),
        pltpu.VMEM((HEADS, 3, TILE, TILE), BF16),
        pltpu.VMEM((GROUPS, DH, DH), F32),
        pltpu.VMEM((3, GROUPS, DH, DH), BF16),
        pltpu.VMEM((7, GROUPS, DH, DH), BF16),
        pltpu.VMEM((GROUPS, CROSS * DH, DH), BF16),
        pltpu.VMEM((GROUPS, DH, CROSS * DH), F32),
        pltpu.VMEM((GROUPS, DH, DH), F32),
        pltpu.VMEM((7, GROUPS, DH, DH), BF16),
        pltpu.VMEM((7, GROUPS, DH, DH), BF16),
        pltpu.VMEM((TOKENS, GROUPS * DH), F32),
        pltpu.VMEM((TOKENS, GROUPS * DH), F32),
        pltpu.SemaphoreType.DMA((7,)),
        pltpu.SemaphoreType.DMA((COPIES,)),
        pltpu.SemaphoreType.DMA((COPIES,)),
    ]
    hbm = pl.BlockSpec(memory_space=pl.ANY)
    shapes = (
        ((TOKENS, WIDTH), BF16),
        ((TOKENS, WIDTH), BF16),
        ((TOKENS, GROUPS * DH), BF16),
        ((TOKENS, GROUPS * DH), BF16),
        ((CH, WIDTH), F32),
    )
    results = pl.pallas_call(
        make_kernel(norm),
        out_shape=tuple(pltpu.VMEM(*shape) for shape in shapes),
        in_specs=[hbm] * 7,
        out_specs=(vmem,) * 5,
        scratch_shapes=scratch,
        compiler_params=pltpu.CompilerParams(
            collective_id=0, has_side_effects=True, vmem_limit_bytes=56 << 20
        ),
        name="layer",
    )(
        queries,
        key_heads,
        value_heads,
        class_ids.reshape(1, tokens),
        level_table.transpose(2, 1, 0),
        out_weight,
        out_grad,
    )
    return pl.pallas_call(
        store,
        out_shape=tuple(jax.ShapeDtypeStruct(*shape) for shape in shapes),
        in_specs=[vmem] * 5,
        out_specs=(pl.BlockSpec(memory_space=pl.ANY),) * 5,
        scratch_shapes=[pltpu.SemaphoreType.DMA((5,))],
        name="store",
    )(*(pltpu.with_memory_space_constraint(result, pltpu.VMEM) for result in results))


def solution(mesh):
    placed = (
        P("ctx", "heads"),
        P("ctx", "heads"),
        P("ctx", "heads"),
        P("ctx"),
        P(None, "heads", None),
        P("ctx", "heads"),
        P("ctx", "heads"),
    )
    return jax.shard_map(
        local,
        mesh=mesh,
        in_specs=placed,
        out_specs=(P("ctx", "heads"),) * 5,
        check_vma=False,
    )
```
